256 devices in a mesh: ax: 64 (over x, y, z_lo, core), az: 4 (over z_hi).
Axes of the slice: x: 4, y: 4, z: 8 (z_hi: 4, z_lo: 2; z = z_hi * 2 + z_lo), core: 2. Of those that a mesh axis runs over, the one named last changes fastest.
Arguments:
- phase_field: float32 [1024, 256, 512], P('ax', None, 'az'), may hold values from -6 to 6
- section_cotangent: float32 [1024, 256, 512], P('ax', None, 'az'), may hold values from -6 to 6
Outputs:
- phase_gradient: float32 [1024, 256, 512], P('ax', None, 'az')
The draws below stay inside these ranges and needn't reach their ends.
All inputs are finite; a program needn't handle non-finite values.
Results may differ from the reference program's by a relative error of at most 0.00012.
Values sent between devices are 32-bit elements; how exact they have to be, the bound alone decides.
No kernel may reach another device: no remote copies, remote signals or barrier semaphores. Data moves between devices by JAX's collectives and lax.ppermute only.
A program may use at most 64 MiB of HBM per device.

```python
import math
import jax
import jax.numpy as jnp
from jax import lax

NX = 1024
NY = 512
NR = 256


def levels(rng, extent, split, low, high):
    level = 1.0
    for position, blocks in split:
        heights = jax.random.uniform(jax.random.fold_in(jax.random.fold_in(rng, 6), position), (blocks,), jnp.float32, low / len(split), high / len(split))
        level = level * jnp.repeat(jnp.exp(heights), extent[position] // blocks).reshape((-1,) + (1,) * (len(extent) - 1 - position))
    return level


def bell_draw(own_key, shape, deviation, limit, split=(), kind=jnp.bfloat16):
    drawn = jax.random.normal(own_key, shape, jnp.float32) * deviation
    if len(split) > 0:
        drawn = levels(own_key, shape, split, -0.22, 0.18) * drawn
    return jnp.clip(drawn, min=-limit, max=limit).astype(kind)


def setup_inputs(seed: int = 0) -> dict:
    splits = jax.random.split(jax.random.key(seed), 3)
    phase_field = bell_draw(splits[0], (NX, NR, NY), 1.0, 6.0, ((0, 64), (2, 4)), jnp.float32)
    section_cotangent = bell_draw(splits[1], (NX, NR, NY), 1.0, 6.0, ((0, 64), (2, 4)), jnp.float32)
    return {"phase_field": phase_field, "section_cotangent": section_cotangent}


def radial_table(count):
    modes = jnp.arange(count, dtype=jnp.float32)[:, None]
    points = jnp.arange(count, dtype=jnp.float32)[None, :]
    weight = jnp.where(modes == 0, math.sqrt(1.0 / count), math.sqrt(2.0 / count))
    return weight * jnp.cos(math.pi * modes * (points + 0.5) / count)

def fourier_synthesis(coeffs, axis):
    moved = jnp.moveaxis(coeffs, axis, -1)
    count = moved.shape[-1]
    half = count // 2
    root = math.sqrt(count)
    root_half = math.sqrt(count / 2.0)
    real_part = jnp.concatenate([moved[..., :1] * root, moved[..., 1:half] * root_half, moved[..., half:half + 1] * root], axis=-1)
    imag_part = jnp.concatenate([jnp.zeros_like(moved[..., :1]), -moved[..., half + 1:] * root_half, jnp.zeros_like(moved[..., :1])], axis=-1)
    values = jnp.fft.irfft(lax.complex(real_part, imag_part), n=count, axis=-1)
    return jnp.moveaxis(values.astype(coeffs.dtype), -1, axis)

def fourier_analysis(values, axis):
    moved = jnp.moveaxis(values, axis, -1)
    count = moved.shape[-1]
    half = count // 2
    root = math.sqrt(count)
    scale = math.sqrt(2.0 / count)
    spectrum = jnp.fft.rfft(moved, axis=-1)
    real_part = jnp.real(spectrum).astype(values.dtype)
    imag_part = jnp.imag(spectrum).astype(values.dtype)
    coeffs = jnp.concatenate([real_part[..., :1] / root, real_part[..., 1:half] * scale, real_part[..., half:half + 1] / root, -imag_part[..., 1:half] * scale], axis=-1)
    return jnp.moveaxis(coeffs, -1, axis)

def reference(phase_field, section_cotangent):
    table = radial_table(NR)
    highest = lax.Precision.HIGHEST

    def to_grid(coeffs):
        radial = jnp.einsum('xmy,mj->xjy', coeffs, table, precision=highest)
        return fourier_synthesis(fourier_synthesis(radial, 2), 0)
    state = to_grid(phase_field)
    adjoint = to_grid(section_cotangent)
    weighted = (3.0 * state * state - 1.0) * adjoint
    spectral = fourier_analysis(fourier_analysis(weighted, 0), 2)
    return jnp.einsum('xjy,mj->xmy', spectral, table, precision=highest)
```

```python
import functools
import math

import jax
import jax.numpy as jnp
import ml_dtypes
import numpy as np
from jax import lax
from jax.experimental import pallas as pl
from jax.experimental.pallas import tpu as pltpu
from jax.sharding import PartitionSpec as P

NX = 1024
NY = 512
NR = 256
BOTH = ("ax", "az")


def halves(table):
    high = table.astype(ml_dtypes.bfloat16)
    low = (table - high.astype(np.float64)).astype(ml_dtypes.bfloat16)
    return high, low


def fourier_table(count):
    modes = np.arange(count)[:, None]
    points = np.arange(count)[None, :]
    half = count // 2
    wave = np.where(modes <= half, modes, modes - half)
    angle = 2.0 * math.pi / count * (wave * points % count)
    scale = np.where((modes == 0) | (modes == half), math.sqrt(1.0 / count), math.sqrt(2.0 / count))
    return scale * np.where(modes <= half, np.cos(angle), np.sin(angle))


def radial_table(count):
    modes = np.arange(count)[:, None]
    points = np.arange(count)[None, :]
    weight = np.where(modes == 0, math.sqrt(1.0 / count), math.sqrt(2.0 / count))
    return weight * np.cos(math.pi * modes * (points + 0.5) / count)


def split(x):
    high = x.astype(jnp.bfloat16)
    low = (x - high.astype(jnp.float32)).astype(jnp.bfloat16)
    return high, low


def product(a, b, dims):
    dot = functools.partial(
        lax.dot_general, dimension_numbers=(dims, ((), ())), preferred_element_type=jnp.float32
    )
    return dot(a[0], b[0]) + (dot(a[0], b[1]) + dot(a[1], b[0]))


NN = ((1,), (0,))
NT = ((1,), (1,))


def radial_out(s_ref, a_ref, th_ref, tl_ref, out_ref):
    step = pl.program_id(0)
    table = th_ref[...], tl_ref[...]

    def synthesize(ref, group):
        for i in range(0, 8, 2):
            pair = jnp.concatenate([ref[i, 0], ref[i + 1, 0]], axis=1)
            result = product(table, split(pair), NN)
            out_ref[pl.ds(group * 8 + i, NR, stride=32), :] = result[:, :128]
            out_ref[pl.ds(group * 8 + i + 1, NR, stride=32), :] = result[:, 128:]

    for group in range(4):

        @pl.when(step == group)
        def _():
            synthesize(s_ref if group < 2 else a_ref, group)


def radial_back(in_ref, th_ref, tl_ref, out_ref):
    step = pl.program_id(0)
    table = th_ref[...], tl_ref[...]
    for parity in range(2):

        @pl.when(step == parity)
        def _():
            for i in range(0, 8, 2):
                row = parity * 8 + i
                pair = jnp.concatenate(
                    [in_ref[pl.ds(row, NR, stride=16), :], in_ref[pl.ds(row + 1, NR, stride=16), :]],
                    axis=1,
                )
                result = product(table, split(pair), NN)
                out_ref[i, 0] = result[:, :128]
                out_ref[i + 1, 0] = result[:, 128:]


def grid_kernel(
    in_ref, yh_ref, yl_ref, eh_ref, el_ref, oh_ref, ol_ref, pth_ref, ptl_ref, out_ref,
    high_ref, low_ref, state_ref, work_ref,
):
    half = NX // 2
    root = math.sqrt(0.5)

    def synthesis(field):
        for chunk in range(2):
            parts = []
            for parity in range(2):
                lanes = [
                    in_ref[:, 2 * chunk + k, field, parity].reshape(half, 128) for k in range(2)
                ]
                x = split(jnp.concatenate(lanes, axis=1))
                table = (eh_ref, el_ref) if parity == 0 else (oh_ref, ol_ref)
                parts.append(product((table[0][...], table[1][...]), x, NN))
            even, odd = parts
            columns = pl.ds(256 * chunk, 256)
            for k, value in enumerate((even + odd, even - odd)):
                high, low = split(value)
                high_ref[pl.ds(half * k, half), columns] = high
                low_ref[pl.ds(half * k, half), columns] = low

    def azimuth_synthesis(rows):
        lines = high_ref[rows, :], low_ref[rows, :]
        return product(lines, (yh_ref[...], yl_ref[...]), NN)

    synthesis(0)

    @pl.loop(0, 4)
    def _(i):
        rows = pl.ds(pl.multiple_of(i * 256, 256), 256)
        state_ref[rows, :] = azimuth_synthesis(rows)

    synthesis(1)

    @pl.loop(0, 4)
    def _(i):
        rows = pl.ds(pl.multiple_of(i * 256, 256), 256)
        state = state_ref[rows, :]
        work_ref[rows, :] = (3.0 * state * state - 1.0) * azimuth_synthesis(rows)

    for chunk in range(2):
        columns = pl.ds(256 * chunk, 256)
        first = work_ref[pl.ds(0, half), columns]
        second = work_ref[pl.ds(half, half), columns]
        even = product((yh_ref[...], yl_ref[...]), split((first + second) * root), NN)
        odd = product((pth_ref[...], ptl_ref[...]), split(first - second), NN)
        for k, value in enumerate((even, odd)):
            high, low = split(value)
            high_ref[pl.ds(half * k, half), columns] = high
            low_ref[pl.ds(half * k, half), columns] = low

    for parity in range(2):

        @pl.loop(0, 2)
        def _(i):
            rows = pl.ds(pl.multiple_of(parity * half + i * 256, 256), 256)
            lines = high_ref[rows, :], low_ref[rows, :]
            result = product(lines, (yh_ref[...], yl_ref[...]), NT)
            for k in range(4):
                block = result[:, 128 * k : 128 * (k + 1)].reshape(32, 8, 128)
                out_ref[pl.ds(pl.multiple_of(i * 32, 32), 32), k, parity] = block


def whole():
    return pl.BlockSpec(memory_space=pltpu.VMEM)


def params(**more):
    return pltpu.CompilerParams(vmem_limit_bytes=56 * 2**20, **more)


def per_device(phase_field, section_cotangent):
    radial = radial_table(NR)
    azimuth = fourier_table(NY)
    axial = fourier_table(NX)
    ch, cl = halves(radial)
    cth, ctl = halves(np.ascontiguousarray(radial.T))
    yh, yl = halves(azimuth)
    eh, el = halves(np.ascontiguousarray(axial[0::2, : NX // 2].T))
    ph, plow = halves(np.ascontiguousarray(axial[1::2, : NX // 2].T))
    pth, ptl = halves(np.ascontiguousarray(axial[1::2, : NX // 2]))

    s = phase_field.reshape(8, 2, NR, 128)
    a = section_cotangent.reshape(8, 2, NR, 128)
    table_spec = pl.BlockSpec((NR, NR), lambda g: (0, 0))
    sent = pl.pallas_call(
        radial_out,
        grid=(4,),
        in_specs=[
            pl.BlockSpec((8, 1, NR, 128), lambda g: (0, jnp.minimum(g, 1), 0, 0)),
            pl.BlockSpec((8, 1, NR, 128), lambda g: (0, jnp.maximum(g - 2, 0), 0, 0)),
            table_spec,
            table_spec,
        ],
        out_specs=pl.BlockSpec((NR * 32, 128), lambda g: (0, 0)),
        out_shape=jax.ShapeDtypeStruct((NR * 32, 128), jnp.float32),
        compiler_params=params(),
        name="radial_out",
    )(s, a, cth, ctl)
    taken = lax.all_to_all(sent.reshape(NR, 32, 128), BOTH, split_axis=0, concat_axis=0, tiled=True)
    weighted = pl.pallas_call(
        grid_kernel,
        in_specs=[whole()] * 9,
        out_specs=whole(),
        out_shape=jax.ShapeDtypeStruct((64, 4, 2, 8, 128), jnp.float32),
        scratch_shapes=[
            pltpu.VMEM((NX, NY), jnp.bfloat16),
            pltpu.VMEM((NX, NY), jnp.bfloat16),
            pltpu.VMEM((NX, NY), jnp.float32),
            pltpu.VMEM((NX, NY), jnp.float32),
        ],
        compiler_params=params(),
        name="grid",
    )(taken.reshape(64, 4, 2, 2, 8, 128), yh, yl, eh, el, ph, plow, pth, ptl)
    back = lax.all_to_all(weighted.reshape(NR, 16, 128), BOTH, split_axis=0, concat_axis=0, tiled=True)
    gradient = pl.pallas_call(
        radial_back,
        grid=(2,),
        in_specs=[pl.BlockSpec((NR * 16, 128), lambda g: (0, 0)), table_spec, table_spec],
        out_specs=pl.BlockSpec((8, 1, NR, 128), lambda g: (0, g, 0, 0)),
        out_shape=jax.ShapeDtypeStruct((8, 2, NR, 128), jnp.float32),
        compiler_params=params(),
        name="radial_back",
    )(back.reshape(NR * 16, 128), ch, cl)
    return gradient.reshape(16, NR, 128)


def solution(mesh):
    spec = P("ax", None, "az")
    return jax.shard_map(
        per_device, mesh=mesh, in_specs=(spec, spec), out_specs=spec, check_vma=False
    )
```

```python
import functools
import math

import jax
import jax.numpy as jnp
import ml_dtypes
import numpy as np
from jax import lax
from jax.experimental import pallas as pl
from jax.experimental.pallas import tpu as pltpu
from jax.sharding import Mesh, PartitionSpec as P

NX = 1024
NY = 512
NR = 256
AXES = ("x", "y", "zl", "co", "zh")
SHARD = ("x", "y", "zl", "co")
RING = ("zl", "zh")
PLANE = ("x", "y", "co")
OFFSETS = (3, 5, 4, 2, 6, 1, 7)


def halves(table):
    high = table.astype(ml_dtypes.bfloat16)
    low = (table - high.astype(np.float64)).astype(ml_dtypes.bfloat16)
    return high, low


def fourier_table(count):
    modes = np.arange(count)[:, None]
    points = np.arange(count)[None, :]
    half = count // 2
    wave = np.where(modes <= half, modes, modes - half)
    angle = 2.0 * math.pi / count * (wave * points % count)
    scale = np.where((modes == 0) | (modes == half), math.sqrt(1.0 / count), math.sqrt(2.0 / count))
    return scale * np.where(modes <= half, np.cos(angle), np.sin(angle))


def radial_table(count):
    modes = np.arange(count)[:, None]
    points = np.arange(count)[None, :]
    weight = np.where(modes == 0, math.sqrt(1.0 / count), math.sqrt(2.0 / count))
    return weight * np.cos(math.pi * modes * (points + 0.5) / count)


def split(x):
    high = x.astype(jnp.bfloat16)
    low = (x - high.astype(jnp.float32)).astype(jnp.bfloat16)
    return high, low


def product(a, b, dims):
    dot = functools.partial(
        lax.dot_general, dimension_numbers=(dims, ((), ())), preferred_element_type=jnp.float32
    )
    return dot(a[0], b[0]) + (dot(a[0], b[1]) + dot(a[1], b[0]))


NN = ((1,), (0,))
NT = ((1,), (1,))


def my_z():
    return 2 * lax.axis_index("zh") + lax.axis_index("zl")


def radial_out(ring_first, z_ref, x_ref, th_ref, tl_ref, *out_refs):
    group = pl.program_id(0)
    rows = pl.ds(pl.multiple_of(z_ref[0] * 32, 32), NR)
    table = th_ref[rows, :], tl_ref[rows, :]
    for i in range(0, 8, 2):
        pair = jnp.concatenate([x_ref[i, 0], x_ref[i + 1, 0]], axis=1)
        result = product(table, split(pair), NN)
        for k in range(2):
            for o in range(8):
                value = result[32 * o : 32 * (o + 1), 128 * k : 128 * (k + 1)]
                row = group * 8 + i + k
                if ring_first:
                    out_refs[o][pl.ds(row, 32, stride=16), :] = value
                else:
                    out_refs[0][pl.ds(16 * o + row, 32, stride=128), :] = value


def merge(*refs):
    for o in range(8):
        refs[8][:, o] = refs[o][...]


def spread(in_ref, *out_refs):
    for o in range(8):
        out_refs[o][...] = in_ref[:, o]


def place(z, value_of, high_ref, low_ref):
    for o in range(8):
        source = lax.rem(z - o + 8, 8)
        rows = pl.ds(pl.multiple_of(lax.rem(source, 2) * 16, 16), 16)
        columns = pl.ds(pl.multiple_of(lax.div(source, 2) * 128, 128), 128)
        for parity in range(2):
            high, low = split(value_of(o, parity).reshape(16, 16, 128))
            high_ref[parity, :, rows, columns] = high
            low_ref[parity, :, rows, columns] = low


def axial_synthesis(xh_ref, xl_ref, tables, high_ref, low_ref):
    half = NX // 2
    for chunk in range(2):
        columns = pl.ds(256 * chunk, 256)
        parts = []
        for parity in range(2):
            th_ref, tl_ref = tables[parity]
            x = [ref[parity, :, :, columns].reshape(half, 256) for ref in (xh_ref, xl_ref)]
            parts.append(product((th_ref[...], tl_ref[...]), x, NN))
        even, odd = parts
        for k, value in enumerate((even + odd, even - odd)):
            high, low = split(value)
            high_ref[pl.ds(half * k, half), columns] = high
            low_ref[pl.ds(half * k, half), columns] = low


def state_kernel(
    z_ref, in_ref, yh_ref, yl_ref, eh_ref, el_ref, oh_ref, ol_ref, state_ref,
    xh_ref, xl_ref, high_ref, low_ref,
):
    place(z_ref[0], lambda o, parity: in_ref[:, o, parity], xh_ref, xl_ref)
    axial_synthesis(xh_ref, xl_ref, ((eh_ref, el_ref), (oh_ref, ol_ref)), high_ref, low_ref)

    @pl.loop(0, 4)
    def _(i):
        rows = pl.ds(pl.multiple_of(i * 256, 256), 256)
        lines = high_ref[rows, :], low_ref[rows, :]
        state_ref[rows, :] = product(lines, (yh_ref[...], yl_ref[...]), NN)


def analysis(z, table, folded, azimuth, store, high_ref, low_ref, result_ref):
    for chunk in range(2):
        value = product(table, folded(pl.ds(256 * chunk, 256)), NN)
        high, low = split(value)
        columns = pl.ds(256 * chunk, 256)
        high_ref[:, columns] = high
        low_ref[:, columns] = low

    @pl.loop(0, 2)
    def _(i):
        rows = pl.ds(pl.multiple_of(i * 256, 256), 256)
        value = product((high_ref[rows, :], low_ref[rows, :]), azimuth, NT)
        result_ref[pl.ds(pl.multiple_of(i * 8, 8), 8)] = value.reshape(8, 2, 16, NY)

    for o in range(8):
        target = lax.rem(z + o, 8)
        columns = pl.ds(pl.multiple_of(lax.div(target, 2) * 128, 128), 128)
        store(o, result_ref[:, lax.rem(target, 2), :, columns].reshape(32, 8, 128))


def grid_kernel(
    z_ref, state_ref, p0, p1, p2, p3, p4, p5, p6, p7,
    yh_ref, yl_ref, eh_ref, el_ref, oh_ref, ol_ref,
    q0, q1, q2, q3, q4, q5, q6, q7, odd_h_ref, odd_l_ref,
    xh_ref, xl_ref, high_ref, low_ref, work_ref, result_ref,
):
    pieces = (p0, p1, p2, p3, p4, p5, p6, p7)
    outs = (q0, q1, q2, q3, q4, q5, q6, q7)
    half = NX // 2
    place(z_ref[0], lambda o, parity: pieces[o][:, parity], xh_ref, xl_ref)
    axial_synthesis(xh_ref, xl_ref, ((eh_ref, el_ref), (oh_ref, ol_ref)), high_ref, low_ref)
    azimuth = yh_ref[...], yl_ref[...]

    @pl.loop(0, 4)
    def _(i):
        rows = pl.ds(pl.multiple_of(i * 256, 256), 256)
        state = state_ref[rows, :]
        adjoint = product((high_ref[rows, :], low_ref[rows, :]), azimuth, NN)
        work_ref[rows, :] = (3.0 * state * state - 1.0) * adjoint

    first, second = pl.ds(0, half), pl.ds(half, half)
    odd_h_ref[...], odd_l_ref[...] = split(work_ref[first, :] - work_ref[second, :])
    root = math.sqrt(0.5)

    def store(o, value):
        outs[o][...] = value

    analysis(
        z_ref[0], azimuth,
        lambda c: split((work_ref[first, c] + work_ref[second, c]) * root), azimuth, store,
        high_ref.at[first], low_ref.at[first], result_ref,
    )


def odd_kernel(
    z_ref, odd_h_ref, odd_l_ref, yh_ref, yl_ref, ph_ref, pl_ref, out_ref, high_ref, low_ref, result_ref
):
    def store(o, value):
        out_ref[:, o] = value

    analysis(
        z_ref[0], (ph_ref[...], pl_ref[...]), lambda c: (odd_h_ref[:, c], odd_l_ref[:, c]),
        (yh_ref[...], yl_ref[...]), store, high_ref, low_ref, result_ref,
    )


def radial_back(merged, z_ref, th_ref, tl_ref, *refs):
    in_refs, (out_ref, high_ref, low_ref) = refs[: 1 if merged else 8], refs[-3:]
    table = th_ref[...], tl_ref[...]
    for i in range(0, 8, 2):
        for o in range(8):
            rows = pl.ds(pl.multiple_of(lax.rem(z_ref[0] - o + 8, 8) * 32, 32), 32)
            for k in range(2):
                if merged:
                    value = in_refs[0][pl.ds(8 * o + i + k, 32, stride=64), :]
                else:
                    value = in_refs[o][pl.ds(i + k, 32, stride=8), :]
                columns = slice(128 * k, 128 * (k + 1))
                high_ref[i // 2, rows, columns], low_ref[i // 2, rows, columns] = split(value)
    for i in range(0, 8, 2):
        result = product(table, (high_ref[i // 2], low_ref[i // 2]), NN)
        out_ref[i, 0] = result[:, :128]
        out_ref[i + 1, 0] = result[:, 128:]


def call(kernel, name, outs, ins, flops=0, scratch=(), **more):
    vmem = pl.BlockSpec(memory_space=pltpu.VMEM)
    size = sum(math.prod(a.shape) * a.dtype.itemsize for a in (*ins[1:], *outs))
    return pl.pallas_call(
        kernel,
        in_specs=more.pop("in_specs", [pl.BlockSpec(memory_space=pltpu.SMEM)] + [vmem] * (len(ins) - 1)),
        out_specs=more.pop("out_specs", [vmem] * len(outs)),
        out_shape=outs,
        scratch_shapes=list(scratch),
        cost_estimate=pl.CostEstimate(flops=flops, bytes_accessed=size, transcendentals=0),
        compiler_params=pltpu.CompilerParams(vmem_limit_bytes=LIMIT),
        name=name,
        **more,
    )(*ins)


LIMIT = 40 * 2**20


def f32(*shape):
    return jax.ShapeDtypeStruct(shape, jnp.float32)


def bf16(*shape):
    return jax.ShapeDtypeStruct(shape, jnp.bfloat16)


def ring_index(z):
    return (z % 2) * 4 + (z % 8) // 2


def ring(pieces):
    out = list(pieces)
    for o in OFFSETS:
        pairs = [(ring_index(z), ring_index(z + o)) for z in range(8)]
        out[o] = lax.ppermute(pieces[o], RING, pairs)
    return out


def plane(x):
    return lax.all_to_all(x, PLANE, split_axis=0, concat_axis=0, tiled=True)


def per_device(phase_field, section_cotangent):
    radial = radial_table(NR)
    axial = fourier_table(NX)
    c = halves(radial)
    ct = halves(np.concatenate([radial.T, radial.T]))
    y = halves(fourier_table(NY))
    e = halves(np.ascontiguousarray(axial[0::2, : NX // 2].T))
    p = halves(np.ascontiguousarray(axial[1::2, : NX // 2].T))
    pt = halves(np.ascontiguousarray(axial[1::2, : NX // 2]))
    z = my_z().astype(jnp.int32).reshape(1)
    point = 2 * 3

    def synthesize(x, ring_first, name):
        outs = [f32(512, 128)] * 8 if ring_first else [f32(4096, 128)]
        table = pl.BlockSpec((2 * NR, NR), lambda g: (0, 0))
        return call(
            functools.partial(radial_out, ring_first), name, outs,
            [z, x.reshape(8, 2, NR, 128), *ct], point * NR * 2**19, grid=(2,),
            in_specs=[
                pl.BlockSpec(memory_space=pltpu.SMEM),
                pl.BlockSpec((8, 1, NR, 128), lambda g: (0, g, 0, 0)), table, table,
            ],
            out_specs=[pl.BlockSpec(o.shape, lambda g: (0, 0)) for o in outs],
        )

    s = synthesize(phase_field, True, "radial_state")
    s = ring(s)
    (a,) = synthesize(section_cotangent, False, "radial_adjoint")
    a = plane(a.reshape(32, 8, 16, 128))
    a = pl.pallas_call(
        spread, in_specs=[pl.BlockSpec(memory_space=pltpu.VMEM)],
        out_specs=[pl.BlockSpec(memory_space=pltpu.VMEM)] * 8, out_shape=[f32(32, 16, 128)] * 8,
        name="spread_adjoint",
    )(a)
    a = ring(a)

    def merged(pieces, name):
        rows = pieces[0].shape[1]
        return pl.pallas_call(
            merge, in_specs=[pl.BlockSpec(memory_space=pltpu.VMEM)] * 8,
            out_specs=pl.BlockSpec(memory_space=pltpu.VMEM), out_shape=f32(32, 8, rows, 128), name=name,
        )(*pieces)

    s = plane(merged([v.reshape(32, 16, 128) for v in s], "merge_state"))
    places = [pltpu.VMEM((2, 16, 32, NY), jnp.bfloat16)] * 2
    lines = [pltpu.VMEM((NX, NY), jnp.bfloat16)] * 2
    small = [pltpu.VMEM((NX // 2, NY), jnp.bfloat16)] * 2
    result = pltpu.VMEM((16, 2, 16, NY), jnp.float32)
    (state,) = call(
        state_kernel, "state", [f32(NX, NY)], [z, s.reshape(32, 8, 2, 8, 128), *y, *e, *p],
        point * 1024 * 2**19, scratch=places + lines,
    )
    *even, odd_h, odd_l = call(
        grid_kernel, "grid", [f32(32, 8, 128)] * 8 + [bf16(NX // 2, NY)] * 2,
        [z, state, *(v.reshape(32, 2, 8, 128) for v in a), *y, *e, *p], point * 1536 * 2**19,
        scratch=places + lines + [pltpu.VMEM((NX, NY), jnp.float32), result],
    )
    even = ring(even)
    (odd,) = call(
        odd_kernel, "odd", [f32(32, 8, 8, 128)], [z, odd_h, odd_l, *y, *pt], point * 512 * 2**19,
        scratch=small + [result],
    )
    odd = plane(odd)
    odd = pl.pallas_call(
        spread, in_specs=[pl.BlockSpec(memory_space=pltpu.VMEM)],
        out_specs=[pl.BlockSpec(memory_space=pltpu.VMEM)] * 8, out_shape=[f32(32, 8, 128)] * 8,
        name="spread_odd",
    )(odd)
    odd = ring(odd)
    even = plane(merged(even, "merge_even"))

    def back(pieces, parity, before, name):
        ins = [z, *c, *pieces]
        vmem = pl.BlockSpec(memory_space=pltpu.VMEM)
        specs = [pl.BlockSpec(memory_space=pltpu.SMEM)] + [vmem] * (len(ins) - 1)
        kernel = functools.partial(radial_back, len(pieces) == 1)
        more = {}
        if before is not None:
            body, count = kernel, len(ins)
            kernel = lambda *refs: body(*refs[:count], *refs[count + 1 :])
            more = {"input_output_aliases": {count: 0}}
            ins.append(before)
            specs.append(pl.BlockSpec(memory_space=pl.ANY))
        return call(
            kernel, name, [f32(8, 2, NR, 128)], ins, point * 128 * 2**19, grid=(1,),
            in_specs=specs,
            out_specs=[pl.BlockSpec((8, 1, NR, 128), lambda g: (0, parity, 0, 0))],
            scratch=[pltpu.VMEM((4, NR, 256), jnp.bfloat16)] * 2, **more,
        )[0]

    out = back([even.reshape(2048, 128)], 0, None, "radial_even")
    out = back([v.reshape(256, 128) for v in odd], 1, out, "radial_odd")
    return out.reshape(16, NR, 128)


def solution(mesh):
    names = Mesh(mesh.devices.reshape(4, 4, 2, 2, 4), AXES)
    spec = P(SHARD, None, "zh")
    return jax.shard_map(
        per_device, mesh=names, in_specs=(spec, spec), out_specs=spec, check_vma=False
    )
```

```python
import functools
import math

import jax
import jax.numpy as jnp
import ml_dtypes
import numpy as np
from jax import lax
from jax.experimental import pallas as pl
from jax.experimental.pallas import tpu as pltpu
from jax.sharding import PartitionSpec as P

NX = 1024
NY = 512
NR = 256
BOTH = ("ax", "az")


def halves(table):
    high = table.astype(ml_dtypes.bfloat16)
    low = (table - high.astype(np.float64)).astype(ml_dtypes.bfloat16)
    return high, low


def fourier_table(count):
    modes = np.arange(count)[:, None]
    points = np.arange(count)[None, :]
    half = count // 2
    wave = np.where(modes <= half, modes, modes - half)
    angle = 2.0 * math.pi / count * (wave * points % count)
    scale = np.where((modes == 0) | (modes == half), math.sqrt(1.0 / count), math.sqrt(2.0 / count))
    return scale * np.where(modes <= half, np.cos(angle), np.sin(angle))


def radial_table(count):
    modes = np.arange(count)[:, None]
    points = np.arange(count)[None, :]
    weight = np.where(modes == 0, math.sqrt(1.0 / count), math.sqrt(2.0 / count))
    return weight * np.cos(math.pi * modes * (points + 0.5) / count)


def split(x):
    high = x.astype(jnp.bfloat16)
    low = (x - high.astype(jnp.float32)).astype(jnp.bfloat16)
    return high, low


def dot(a, b):
    return lax.dot_general(a, b, (((1,), (0,)), ((), ())), preferred_element_type=jnp.float32)


def product(a, b):
    return dot(a[0], b[0]) + (dot(a[0], b[1]) + dot(a[1], b[0]))


HALF = NX // 2


def radial_out(s_ref, a_ref, th_ref, tl_ref, out_ref):
    step = pl.program_id(0)
    table = th_ref[...], tl_ref[...]
    rows = out_ref.reshape(NR * 8, 128)

    def synthesize(ref):
        for i in range(0, 8, 2):
            pair = jnp.concatenate([ref[i, 0], ref[i + 1, 0]], axis=1)
            result = product(table, split(pair))
            rows[pl.ds(i, NR, stride=8), :] = result[:, :128]
            rows[pl.ds(i + 1, NR, stride=8), :] = result[:, 128:]

    pl.when(step < 2)(lambda: synthesize(s_ref))
    pl.when(step >= 2)(lambda: synthesize(a_ref))


def radial_back(in_ref, th_ref, tl_ref, out_ref):
    table = th_ref[...], tl_ref[...]
    rows = in_ref.reshape(NR * 8, 128)
    for i in range(0, 8, 2):
        pair = jnp.concatenate(
            [rows[pl.ds(i, NR, stride=8), :], rows[pl.ds(i + 1, NR, stride=8), :]], axis=1
        )
        result = product(table, split(pair))
        out_ref[i, 0] = result[:, :128]
        out_ref[i + 1, 0] = result[:, 128:]


def grid_kernel(
    in_hbm, yh_hbm, yl_hbm, eh_hbm, el_hbm, oh_hbm, ol_hbm, ph_hbm, pl_hbm, out_hbm,
    x_ref, out_ref, table_ref, high_ref, low_ref, state_ref, sems,
):
    tables = (eh_hbm, el_hbm, oh_hbm, ol_hbm, yh_hbm, yl_hbm, ph_hbm, pl_hbm)
    loads = {}
    for n, name in enumerate("eeooyypp"):
        copy = pltpu.make_async_copy(tables[n], table_ref.at[n], sems.at[n])
        loads.setdefault(name, []).append(copy)
    for field in range(2):
        for chunk in range(2):
            blocks = slice(2 * chunk, 2 * chunk + 2)
            loads[field, chunk] = [
                pltpu.make_async_copy(
                    in_hbm.at[:, blocks, field], x_ref.at[field, :, blocks],
                    sems.at[8 + 2 * field + chunk],
                )
            ]
    order = ((0, 0), "e", "o", (0, 1), "y", (1, 0), (1, 1), "p")
    for name in order:
        for copy in loads[name]:
            copy.start()

    def ready(name):
        for copy in loads[name]:
            copy.wait()

    even_table = lambda: (table_ref[0], table_ref[1])
    odd_table = lambda: (table_ref[2], table_ref[3])
    azimuth_table = lambda: (table_ref[4], table_ref[5])
    odd_back_table = lambda: (table_ref[6], table_ref[7])

    def axial_synthesis(field):
        for chunk in range(2):
            ready((field, chunk))
            parts = []
            for parity, table in enumerate((even_table, odd_table)):
                lanes = [
                    x_ref[field, :, 2 * chunk + k, parity].reshape(HALF, 128) for k in range(2)
                ]
                if field == 0 and chunk == 0:
                    ready("eo"[parity])
                parts.append(product(table(), split(jnp.concatenate(lanes, axis=1))))
            even, odd = parts
            columns = pl.ds(256 * chunk, 256)
            for k, value in enumerate((even + odd, even - odd)):
                rows = pl.ds(HALF * k, HALF)
                high_ref[rows, columns], low_ref[rows, columns] = split(value)

    def azimuth_synthesis(k):
        rows = pl.ds(HALF * k, HALF)
        return product((high_ref[rows, :], low_ref[rows, :]), azimuth_table())

    axial_synthesis(0)
    ready("y")
    for k in range(2):
        state_ref[pl.ds(HALF * k, HALF), :] = azimuth_synthesis(k)
    axial_synthesis(1)
    for k in range(2):
        rows = pl.ds(HALF * k, HALF)
        state = state_ref[rows, :]
        state_ref[rows, :] = (3.0 * state * state - 1.0) * azimuth_synthesis(k)
    first, second = pl.ds(0, HALF), pl.ds(HALF, HALF)
    stores = []
    for parity in range(2):
        for chunk in range(2):
            columns = pl.ds(256 * chunk, 256)
            upper, lower = state_ref[first, columns], state_ref[second, columns]
            if parity == 0:
                value = product(azimuth_table(), split(upper + lower))
            else:
                if chunk == 0:
                    ready("p")
                value = product(odd_back_table(), split(upper - lower))
            high_ref[first, columns], low_ref[first, columns] = split(value)
        result = product((high_ref[first, :], low_ref[first, :]), even_table())
        for k in range(4):
            out_ref[:, k, parity] = result[:, 128 * k : 128 * (k + 1)].reshape(64, 8, 128)
        copy = pltpu.make_async_copy(
            out_ref.at[:, :, parity], out_hbm.at[:, :, parity], sems.at[12 + parity]
        )
        copy.start()
        stores.append(copy)
    for copy in stores:
        copy.wait()


PARAMS = pltpu.CompilerParams(vmem_limit_bytes=56 * 2**20)


def run_radial_out(phase_field, section_cotangent):
    ch, cl = halves(np.ascontiguousarray(radial_table(NR).T))
    table = pl.BlockSpec((NR, NR), lambda g: (0, 0))
    return pl.pallas_call(
        radial_out,
        grid=(4,),
        in_specs=[
            pl.BlockSpec((8, 1, NR, 128), lambda g: (0, jnp.minimum(g, 1), 0, 0)),
            pl.BlockSpec((8, 1, NR, 128), lambda g: (0, jnp.maximum(g - 2, 0), 0, 0)),
            table,
            table,
        ],
        out_specs=pl.BlockSpec((NR, 8, 128), lambda g: (0, g, 0)),
        out_shape=jax.ShapeDtypeStruct((NR, 32, 128), jnp.float32),
        compiler_params=PARAMS,
        name="radial_out",
    )(phase_field.reshape(8, 2, NR, 128), section_cotangent.reshape(8, 2, NR, 128), ch, cl)


def run_grid(taken):
    axial = fourier_table(NX)
    y = halves(fourier_table(NY))
    e = halves(np.ascontiguousarray(axial[0::2, :HALF].T))
    o = halves(np.ascontiguousarray(axial[1::2, :HALF].T))
    p = halves(np.ascontiguousarray(axial[1::2, :HALF]) * math.sqrt(2.0))
    anywhere = pl.BlockSpec(memory_space=pl.ANY)
    return pl.pallas_call(
        grid_kernel,
        in_specs=[anywhere] * 9,
        out_specs=anywhere,
        out_shape=jax.ShapeDtypeStruct((64, 4, 2, 8, 128), jnp.float32),
        scratch_shapes=[
            pltpu.VMEM((2, 64, 4, 2, 8, 128), jnp.float32),
            pltpu.VMEM((64, 4, 2, 8, 128), jnp.float32),
            pltpu.VMEM((8, HALF, HALF), jnp.bfloat16),
            pltpu.VMEM((NX, NY), jnp.bfloat16),
            pltpu.VMEM((NX, NY), jnp.bfloat16),
            pltpu.VMEM((NX, NY), jnp.float32),
            pltpu.SemaphoreType.DMA((14,)),
        ],
        compiler_params=PARAMS,
        name="grid",
    )(taken.reshape(64, 4, 2, 2, 8, 128), *y, *e, *o, *p)


def run_radial_back(back):
    ch, cl = halves(radial_table(NR))
    table = pl.BlockSpec((NR, NR), lambda g: (0, 0))
    return pl.pallas_call(
        radial_back,
        grid=(2,),
        in_specs=[pl.BlockSpec((NR, 8, 128), lambda g: (0, g, 0)), table, table],
        out_specs=pl.BlockSpec((8, 1, NR, 128), lambda g: (0, g, 0, 0)),
        out_shape=jax.ShapeDtypeStruct((8, 2, NR, 128), jnp.float32),
        compiler_params=PARAMS,
        name="radial_back",
    )(back, ch, cl).reshape(16, NR, 128)


def exchange(x):
    return lax.all_to_all(x, BOTH, split_axis=0, concat_axis=0, tiled=True)


def per_device(phase_field, section_cotangent):
    taken = exchange(run_radial_out(phase_field, section_cotangent))
    back = exchange(run_grid(taken).reshape(NR, 16, 128))
    return run_radial_back(back)


def solution(mesh):
    spec = P("ax", None, "az")
    return jax.shard_map(
        per_device, mesh=mesh, in_specs=(spec, spec), out_specs=spec, check_vma=False
    )
```

```python
import functools
import math

import jax
import jax.numpy as jnp
import ml_dtypes
import numpy as np
from jax import lax
from jax.experimental import pallas as pl
from jax.experimental.pallas import tpu as pltpu
from jax.sharding import PartitionSpec as P

NX = 1024
NY = 512
NR = 256
BOTH = ("ax", "az")


def halves(table):
    high = table.astype(ml_dtypes.bfloat16)
    low = (table - high.astype(np.float64)).astype(ml_dtypes.bfloat16)
    return high, low


def fourier_table(count):
    modes = np.arange(count)[:, None]
    points = np.arange(count)[None, :]
    half = count // 2
    wave = np.where(modes <= half, modes, modes - half)
    angle = 2.0 * math.pi / count * (wave * points % count)
    scale = np.where((modes == 0) | (modes == half), math.sqrt(1.0 / count), math.sqrt(2.0 / count))
    return scale * np.where(modes <= half, np.cos(angle), np.sin(angle))


def radial_table(count):
    modes = np.arange(count)[:, None]
    points = np.arange(count)[None, :]
    weight = np.where(modes == 0, math.sqrt(1.0 / count), math.sqrt(2.0 / count))
    return weight * np.cos(math.pi * modes * (points + 0.5) / count)


def split(x):
    high = x.astype(jnp.bfloat16)
    low = (x - high.astype(jnp.float32)).astype(jnp.bfloat16)
    return high, low


def dot(a, b):
    return lax.dot_general(a, b, (((1,), (0,)), ((), ())), preferred_element_type=jnp.float32)


def product(a, b):
    return dot(a[0], b[0]) + (dot(a[0], b[1]) + dot(a[1], b[0]))


HALF = NX // 2


def radial_out(s_hbm, a_hbm, th_hbm, tl_hbm, out_ref, x_ref, turn_ref, table_ref, sems):
    tables = [
        pltpu.make_async_copy(th_hbm, table_ref.at[0], sems.at[4]),
        pltpu.make_async_copy(tl_hbm, table_ref.at[1], sems.at[5]),
    ]
    loads = [
        pltpu.make_async_copy((s_hbm, a_hbm)[g // 2].at[:, g % 2], x_ref.at[g], sems.at[g])
        for g in range(4)
    ]
    for copy in (*tables, *loads):
        copy.start()
    for copy in tables:
        copy.wait()
    table = table_ref[0], table_ref[1]
    for g in range(4):
        rows = turn_ref.at[g].reshape(NR * 8, 128)
        loads[g].wait()
        for i in range(0, 8, 2):
            pair = jnp.concatenate([x_ref[g, i], x_ref[g, i + 1]], axis=1)
            result = product(table, split(pair))
            for k in range(2):
                columns = slice(128 * k, 128 * (k + 1))
                rows[pl.ds(i + k, NR, stride=8), :] = result[:, columns]
        out_ref[:, 8 * g : 8 * (g + 1), :] = turn_ref[g]


def radial_back(in_ref, th_ref, tl_ref, out_hbm, out_ref, sems):
    table = th_ref[...], tl_ref[...]
    rows = in_ref.reshape(NR * 16, 128)
    stores = []
    for parity in range(2):
        for i in range(0, 8, 2):
            lanes = [rows[pl.ds(8 * parity + i + k, NR, stride=16), :] for k in range(2)]
            result = product(table, split(jnp.concatenate(lanes, axis=1)))
            for k in range(2):
                out_ref[parity, i + k] = result[:, 128 * k : 128 * (k + 1)]
            stores.append(
                pltpu.make_async_copy(
                    out_ref.at[parity, i : i + 2], out_hbm.at[i : i + 2, parity],
                    sems.at[4 * parity + i // 2],
                )
            )
            stores[-1].start()
    for store in stores:
        store.wait()


def grid_kernel(
    in_ref, yh_ref, yl_ref, eh_ref, el_ref, oh_ref, ol_ref, ph_ref, pl_ref, out_ref,
    high_ref, low_ref, state_ref,
):
    even_table = lambda: (eh_ref[...], el_ref[...])
    odd_table = lambda: (oh_ref[...], ol_ref[...])
    azimuth_table = lambda: (yh_ref[...], yl_ref[...])
    odd_back_table = lambda: (ph_ref[...], pl_ref[...])

    def axial_synthesis(field):
        for chunk in range(2):
            parts = []
            for parity, table in enumerate((even_table, odd_table)):
                lanes = [
                    in_ref[:, 2 * chunk + k, field, parity].reshape(HALF, 128) for k in range(2)
                ]
                parts.append(product(table(), split(jnp.concatenate(lanes, axis=1))))
            even, odd = parts
            columns = pl.ds(256 * chunk, 256)
            for k, value in enumerate((even + odd, even - odd)):
                rows = pl.ds(HALF * k, HALF)
                high_ref[rows, columns], low_ref[rows, columns] = split(value)

    def azimuth_synthesis(k):
        rows = pl.ds(HALF * k, HALF)
        return product((high_ref[rows, :], low_ref[rows, :]), azimuth_table())

    axial_synthesis(0)
    for k in range(2):
        state_ref[pl.ds(HALF * k, HALF), :] = azimuth_synthesis(k)
    axial_synthesis(1)
    for k in range(2):
        rows = pl.ds(HALF * k, HALF)
        state = state_ref[rows, :]
        state_ref[rows, :] = (3.0 * state * state - 1.0) * azimuth_synthesis(k)
    first, second = pl.ds(0, HALF), pl.ds(HALF, HALF)
    for parity in range(2):
        for chunk in range(2):
            columns = pl.ds(256 * chunk, 256)
            upper, lower = state_ref[first, columns], state_ref[second, columns]
            if parity == 0:
                value = product(azimuth_table(), split(upper + lower))
            else:
                value = product(odd_back_table(), split(upper - lower))
            high_ref[first, columns], low_ref[first, columns] = split(value)
        result = product((high_ref[first, :], low_ref[first, :]), even_table())
        for k in range(4):
            out_ref[:, k, parity] = result[:, 128 * k : 128 * (k + 1)].reshape(64, 8, 128)


def params(mebibytes):
    return pltpu.CompilerParams(vmem_limit_bytes=mebibytes * 2**20)


NEAR = pl.BlockSpec(memory_space=pltpu.VMEM)


FAR = pl.BlockSpec(memory_space=pl.ANY)


def far(x):
    return pltpu.with_memory_space_constraint(x, pltpu.HBM)


def near_shape(*dims):
    return pltpu.VMEM(dims, jnp.float32)


def run_radial_out(phase_field, section_cotangent):
    c = halves(np.ascontiguousarray(radial_table(NR).T))
    return pl.pallas_call(
        radial_out,
        in_specs=[FAR] * 4,
        out_specs=NEAR,
        out_shape=near_shape(NR, 32, 128),
        scratch_shapes=[
            pltpu.VMEM((4, 8, NR, 128), jnp.float32),
            pltpu.VMEM((4, NR, 8, 128), jnp.float32),
            pltpu.VMEM((2, NR, NR), jnp.bfloat16),
            pltpu.SemaphoreType.DMA((6,)),
        ],
        compiler_params=params(20),
        name="radial_out",
    )(*(far(x) for x in (phase_field.reshape(8, 2, NR, 128), section_cotangent.reshape(8, 2, NR, 128), *c)))


def run_grid(taken):
    axial = fourier_table(NX)
    y = halves(fourier_table(NY))
    e = halves(np.ascontiguousarray(axial[0::2, :HALF].T))
    o = halves(np.ascontiguousarray(axial[1::2, :HALF].T))
    p = halves(np.ascontiguousarray(axial[1::2, :HALF]) * math.sqrt(2.0))
    return pl.pallas_call(
        grid_kernel,
        in_specs=[NEAR] * 9,
        out_specs=NEAR,
        out_shape=near_shape(64, 4, 2, 8, 128),
        scratch_shapes=[
            pltpu.VMEM((NX, NY), jnp.bfloat16),
            pltpu.VMEM((NX, NY), jnp.bfloat16),
            pltpu.VMEM((NX, NY), jnp.float32),
        ],
        compiler_params=params(30),
        name="grid",
    )(taken.reshape(64, 4, 2, 2, 8, 128), *y, *e, *o, *p)


def run_radial_back(back):
    c = halves(radial_table(NR))
    return pl.pallas_call(
        radial_back,
        in_specs=[NEAR] * 3,
        out_specs=FAR,
        out_shape=jax.ShapeDtypeStruct((8, 2, NR, 128), jnp.float32),
        scratch_shapes=[pltpu.VMEM((2, 8, NR, 128), jnp.float32), pltpu.SemaphoreType.DMA((8,))],
        compiler_params=params(14),
        name="radial_back",
    )(back, *c).reshape(16, NR, 128)


def exchange(x):
    return lax.all_to_all(x, BOTH, split_axis=0, concat_axis=0, tiled=True)


def per_device(phase_field, section_cotangent):
    taken = exchange(run_radial_out(phase_field, section_cotangent))
    back = exchange(run_grid(taken).reshape(NR, 16, 128))
    return run_radial_back(back)


def solution(mesh):
    spec = P("ax", None, "az")
    return jax.shard_map(
        per_device, mesh=mesh, in_specs=(spec, spec), out_specs=spec, check_vma=False
    )
```

```python
import functools
import math

import jax
import jax.numpy as jnp
import ml_dtypes
import numpy as np
from jax import lax
from jax.experimental import pallas as pl
from jax.experimental.pallas import tpu as pltpu
from jax.sharding import PartitionSpec as P

NX = 1024
NY = 512
NR = 256
BOTH = ("ax", "az")


def halves(table):
    high = table.astype(ml_dtypes.bfloat16)
    low = (table - high.astype(np.float64)).astype(ml_dtypes.bfloat16)
    return high, low


def fourier_table(count):
    modes = np.arange(count)[:, None]
    points = np.arange(count)[None, :]
    half = count // 2
    wave = np.where(modes <= half, modes, modes - half)
    angle = 2.0 * math.pi / count * (wave * points % count)
    scale = np.where((modes == 0) | (modes == half), math.sqrt(1.0 / count), math.sqrt(2.0 / count))
    return scale * np.where(modes <= half, np.cos(angle), np.sin(angle))


def radial_table(count):
    modes = np.arange(count)[:, None]
    points = np.arange(count)[None, :]
    weight = np.where(modes == 0, math.sqrt(1.0 / count), math.sqrt(2.0 / count))
    return weight * np.cos(math.pi * modes * (points + 0.5) / count)


def split(x):
    high = x.astype(jnp.bfloat16)
    low = (x - high.astype(jnp.float32)).astype(jnp.bfloat16)
    return high, low


def dot(a, b):
    return lax.dot_general(a, b, (((1,), (0,)), ((), ())), preferred_element_type=jnp.float32)


def product(a, b):
    return dot(a[0], b[0]) + (dot(a[0], b[1]) + dot(a[1], b[0]))


HALF = NX // 2
QUARTER = NX // 4


def radial_out(s_hbm, a_hbm, th_hbm, tl_hbm, out_ref, x_ref, turn_ref, table_ref, sems):
    tables = [
        pltpu.make_async_copy(th_hbm, table_ref.at[0], sems.at[4]),
        pltpu.make_async_copy(tl_hbm, table_ref.at[1], sems.at[5]),
    ]
    loads = [
        pltpu.make_async_copy((s_hbm, a_hbm)[g // 2].at[:, g % 2], x_ref.at[g], sems.at[g])
        for g in range(4)
    ]
    for copy in (*tables, *loads):
        copy.start()
    for copy in tables:
        copy.wait()
    table = table_ref[0], table_ref[1]
    for g in range(4):
        rows = turn_ref.at[g].reshape(NR * 8, 128)
        loads[g].wait()
        for i in range(0, 8, 2):
            pair = jnp.concatenate([x_ref[g, i], x_ref[g, i + 1]], axis=1)
            result = product(table, split(pair))
            for k in range(2):
                columns = slice(128 * k, 128 * (k + 1))
                rows[pl.ds(i + k, NR, stride=8), :] = result[:, columns]
        out_ref[:, 8 * g : 8 * (g + 1), :] = turn_ref[g]


def radial_back(in_ref, th_ref, tl_ref, out_hbm, out_ref, sems):
    table = th_ref[...], tl_ref[...]
    rows = in_ref.reshape(NR * 16, 128)
    stores = []
    for parity in range(2):
        for i in range(0, 8, 2):
            lanes = [rows[pl.ds(8 * parity + i + k, NR, stride=16), :] for k in range(2)]
            result = product(table, split(jnp.concatenate(lanes, axis=1)))
            for k in range(2):
                out_ref[parity, i + k] = result[:, 128 * k : 128 * (k + 1)]
            stores.append(
                pltpu.make_async_copy(
                    out_ref.at[parity, i : i + 2], out_hbm.at[i : i + 2, parity],
                    sems.at[4 * parity + i // 2],
                )
            )
            stores[-1].start()
    for store in stores:
        store.wait()


def axial_tables():
    axial = fourier_table(NX)
    r = np.arange(QUARTER)
    turned = np.where(r == 0, QUARTER, r)
    even, odd = axial[0::2], axial[1::2]
    even_sines = even[QUARTER:, :QUARTER].T.copy()
    even_sines[:, 0] = 0.0
    return even[:QUARTER, :QUARTER].T, even_sines, odd[:QUARTER, :QUARTER].T, odd[QUARTER:][:, turned].T


def grid_kernel(
    in_ref, yh_ref, yl_ref, eh_ref, el_ref, out_table_ref, back_table_ref, out_ref,
    high_ref, low_ref, state_ref,
):
    index = lax.broadcasted_iota(jnp.int32, (QUARTER, 256), 0)
    zero = index == 0
    sign = jnp.where(index % 2 == 0, 1.0, -1.0)
    unit = math.sqrt(1.0 / NX)
    scale = sign * jnp.where(zero, unit, math.sqrt(2.0) * unit)

    def total(x):
        return jnp.sum(x, axis=0, keepdims=True)

    def axial_synthesis(field):
        for chunk in range(2):
            modes = []
            for parity in range(2):
                for part in range(2):
                    axes = slice(32 * part, 32 * (part + 1))
                    lanes = [
                        in_ref[axes, 2 * chunk + k, field, parity].reshape(QUARTER, 128)
                        for k in range(2)
                    ]
                    modes.append(jnp.concatenate(lanes, axis=1))
            ec, es, oc, os = (
                product((out_table_ref[t, 0], out_table_ref[t, 1]), split(modes[t]))
                for t in range(4)
            )
            nyquist = modes[1][0:1] * unit
            middle = total(modes[0] * scale) + nyquist
            ec = ec + sign * nyquist
            even = ec + es, jnp.where(zero, middle, ec - es)
            odd = jnp.where(zero, oc, os + oc), jnp.where(zero, os, os - oc)
            columns = pl.ds(256 * chunk, 256)
            blocks = even[0] + odd[0], even[1] + odd[1], even[0] - odd[0], even[1] - odd[1]
            for k, value in enumerate(blocks):
                rows = pl.ds(QUARTER * k, QUARTER)
                high_ref[rows, columns], low_ref[rows, columns] = split(value)

    def azimuth_synthesis(k):
        rows = pl.ds(HALF * k, HALF)
        return product((high_ref[rows, :], low_ref[rows, :]), (yh_ref[...], yl_ref[...]))

    axial_synthesis(0)
    for k in range(2):
        state_ref[pl.ds(HALF * k, HALF), :] = azimuth_synthesis(k)
    axial_synthesis(1)
    for k in range(2):
        rows = pl.ds(HALF * k, HALF)
        state = state_ref[rows, :]
        state_ref[rows, :] = (3.0 * state * state - 1.0) * azimuth_synthesis(k)

    root = math.sqrt(2.0)

    def back(t, x):
        return product((back_table_ref[t, 0], back_table_ref[t, 1]), split(x))

    for parity in range(2):
        for chunk in range(2):
            columns = pl.ds(256 * chunk, 256)
            w = [state_ref[pl.ds(QUARTER * k, QUARTER), columns] for k in range(4)]
            if parity == 0:
                upper, lower = w[0] + w[2], w[1] + w[3]
                middle = lower[0:1]
                folded = jnp.where(zero, upper, upper + lower)
                cosines = back(0, folded) + (root * scale) * middle
                nyquist = (root * unit) * (total(sign * folded) + middle)
                sines = jnp.where(zero, nyquist, back(1, upper - lower))
            else:
                upper, lower = w[0] - w[2], w[1] - w[3]
                cosines = back(2, jnp.where(zero, upper, upper - lower))
                sines = back(3, jnp.where(zero, lower, upper + lower))
            for k, value in enumerate((cosines, sines)):
                rows = pl.ds(QUARTER * k, QUARTER)
                high_ref[rows, columns], low_ref[rows, columns] = split(value)
        first = pl.ds(0, HALF)
        result = product((high_ref[first, :], low_ref[first, :]), (eh_ref[...], el_ref[...]))
        for k in range(4):
            out_ref[:, k, parity] = result[:, 128 * k : 128 * (k + 1)].reshape(64, 8, 128)


def params(mebibytes):
    return pltpu.CompilerParams(vmem_limit_bytes=mebibytes * 2**20)


NEAR = pl.BlockSpec(memory_space=pltpu.VMEM)


FAR = pl.BlockSpec(memory_space=pl.ANY)


def far(x):
    return pltpu.with_memory_space_constraint(x, pltpu.HBM)


def near_shape(*dims):
    return pltpu.VMEM(dims, jnp.float32)


def run_radial_out(phase_field, section_cotangent):
    c = halves(np.ascontiguousarray(radial_table(NR).T))
    return pl.pallas_call(
        radial_out,
        in_specs=[FAR] * 4,
        out_specs=NEAR,
        out_shape=near_shape(NR, 32, 128),
        scratch_shapes=[
            pltpu.VMEM((4, 8, NR, 128), jnp.float32),
            pltpu.VMEM((4, NR, 8, 128), jnp.float32),
            pltpu.VMEM((2, NR, NR), jnp.bfloat16),
            pltpu.SemaphoreType.DMA((6,)),
        ],
        compiler_params=params(20),
        name="radial_out",
    )(*(far(x.reshape(8, 2, NR, 128)) for x in (phase_field, section_cotangent)), *map(far, c))


def run_grid(taken):
    azimuth = fourier_table(NY)
    y = halves(azimuth)
    e = halves(np.ascontiguousarray(azimuth.T) * math.sqrt(0.5))
    tables = axial_tables()
    out = np.stack([np.stack(halves(t)) for t in tables])
    back = np.stack([np.stack(halves(t.T * math.sqrt(2.0))) for t in tables])
    return pl.pallas_call(
        grid_kernel,
        in_specs=[NEAR] * 7,
        out_specs=NEAR,
        out_shape=near_shape(64, 4, 2, 8, 128),
        scratch_shapes=[
            pltpu.VMEM((NX, NY), jnp.bfloat16),
            pltpu.VMEM((NX, NY), jnp.bfloat16),
            pltpu.VMEM((NX, NY), jnp.float32),
        ],
        compiler_params=params(30),
        name="grid",
    )(taken.reshape(64, 4, 2, 2, 8, 128), *y, *e, out, back)


def run_radial_back(back):
    c = halves(radial_table(NR))
    return pl.pallas_call(
        radial_back,
        in_specs=[NEAR] * 3,
        out_specs=FAR,
        out_shape=jax.ShapeDtypeStruct((8, 2, NR, 128), jnp.float32),
        scratch_shapes=[pltpu.VMEM((2, 8, NR, 128), jnp.float32), pltpu.SemaphoreType.DMA((8,))],
        compiler_params=params(14),
        name="radial_back",
    )(back, *c).reshape(16, NR, 128)


def exchange(x):
    return lax.all_to_all(x, BOTH, split_axis=0, concat_axis=0, tiled=True)


def per_device(phase_field, section_cotangent):
    taken = exchange(run_radial_out(phase_field, section_cotangent))
    back = exchange(run_grid(taken).reshape(NR, 16, 128))
    return run_radial_back(back)


def solution(mesh):
    spec = P("ax", None, "az")
    return jax.shard_map(
        per_device, mesh=mesh, in_specs=(spec, spec), out_specs=spec, check_vma=False
    )
```

```python
import functools
import math

import jax
import jax.numpy as jnp
import ml_dtypes
import numpy as np
from jax import lax
from jax.experimental import pallas as pl
from jax.experimental.pallas import tpu as pltpu
from jax.sharding import PartitionSpec as P

NX = 1024
NY = 512
NR = 256
BOTH = ("ax", "az")


def halves(table):
    high = table.astype(ml_dtypes.bfloat16)
    low = (table - high.astype(np.float64)).astype(ml_dtypes.bfloat16)
    return high, low


def fourier_table(count):
    modes = np.arange(count)[:, None]
    points = np.arange(count)[None, :]
    half = count // 2
    wave = np.where(modes <= half, modes, modes - half)
    angle = 2.0 * math.pi / count * (wave * points % count)
    scale = np.where((modes == 0) | (modes == half), math.sqrt(1.0 / count), math.sqrt(2.0 / count))
    return scale * np.where(modes <= half, np.cos(angle), np.sin(angle))


def radial_table(count):
    modes = np.arange(count)[:, None]
    points = np.arange(count)[None, :]
    weight = np.where(modes == 0, math.sqrt(1.0 / count), math.sqrt(2.0 / count))
    return weight * np.cos(math.pi * modes * (points + 0.5) / count)


def split(x):
    high = x.astype(jnp.bfloat16)
    low = (x - high.astype(jnp.float32)).astype(jnp.bfloat16)
    return high, low


def dot(a, b):
    return lax.dot_general(a, b, (((1,), (0,)), ((), ())), preferred_element_type=jnp.float32)


def product(a, b):
    return dot(a[0], b[0]) + (dot(a[0], b[1]) + dot(a[1], b[0]))


HALF = NX // 2
QUARTER = NX // 4


def radial_out(s_hbm, a_hbm, th_hbm, tl_hbm, out_ref, x_ref, turn_ref, table_ref, sems):
    tables = [
        pltpu.make_async_copy(th_hbm, table_ref.at[0], sems.at[4]),
        pltpu.make_async_copy(tl_hbm, table_ref.at[1], sems.at[5]),
    ]
    loads = [
        pltpu.make_async_copy((s_hbm, a_hbm)[g // 2].at[:, g % 2], x_ref.at[g], sems.at[g])
        for g in range(4)
    ]
    for copy in (*tables, *loads):
        copy.start()
    for copy in tables:
        copy.wait()
    table = table_ref[0], table_ref[1]
    for g in range(4):
        rows = turn_ref.at[g].reshape(NR * 8, 128)
        loads[g].wait()
        for i in range(0, 8, 2):
            pair = jnp.concatenate([x_ref[g, i], x_ref[g, i + 1]], axis=1)
            result = product(table, split(pair))
            for k in range(2):
                columns = slice(128 * k, 128 * (k + 1))
                rows[pl.ds(i + k, NR, stride=8), :] = result[:, columns]
        out_ref[:, 8 * g : 8 * (g + 1), :] = turn_ref[g]


def radial_back(in_ref, th_ref, tl_ref, out_hbm, out_ref, sems):
    table = th_ref[...], tl_ref[...]
    rows = in_ref.reshape(NR * 16, 128)
    stores = []
    for parity in range(2):
        for i in range(0, 8, 2):
            lanes = [rows[pl.ds(8 * parity + i + k, NR, stride=16), :] for k in range(2)]
            result = product(table, split(jnp.concatenate(lanes, axis=1)))
            for k in range(2):
                out_ref[parity, i + k] = result[:, 128 * k : 128 * (k + 1)]
            stores.append(
                pltpu.make_async_copy(
                    out_ref.at[parity, i : i + 2], out_hbm.at[i : i + 2, parity],
                    sems.at[4 * parity + i // 2],
                )
            )
            stores[-1].start()
    for store in stores:
        store.wait()


def axial_tables():
    axial = fourier_table(NX)
    r = np.arange(QUARTER)
    turned = np.where(r == 0, QUARTER, r)
    even, odd = axial[0::2], axial[1::2]
    even_sines = even[QUARTER:, :QUARTER].T.copy()
    even_sines[:, 0] = 0.0
    return even[:QUARTER, :QUARTER].T, even_sines, odd[:QUARTER, :QUARTER].T, odd[QUARTER:][:, turned].T


def azimuth_tables():
    table = fourier_table(NY)
    half = NY // 2
    sines = table[half:, :half].copy()
    sines[0] = 0.0
    return table[:half, :half], sines


def grid_kernel(
    in_ref, line_out_ref, line_back_ref, out_table_ref, back_table_ref, out_ref,
    high_ref, low_ref, state_ref, middle_ref, nyquist_ref,
):
    index = lax.broadcasted_iota(jnp.int32, (QUARTER, 256), 0)
    zero = index == 0
    sign = jnp.where(index % 2 == 0, 1.0, -1.0)
    unit = math.sqrt(1.0 / NX)
    scale = sign * jnp.where(zero, unit, math.sqrt(2.0) * unit)

    lane = lax.broadcasted_iota(jnp.int32, (1, 256), 1)
    lane_zero = lane == 0
    lane_sign = jnp.where(lane % 2 == 0, 1.0, -1.0)
    lane_unit = math.sqrt(1.0 / NY)
    lane_scale = lane_sign * jnp.where(lane_zero, lane_unit, math.sqrt(2.0) * lane_unit)

    def line_total(x):
        return jnp.sum(x, axis=1, keepdims=True)

    def total(x):
        return jnp.sum(x, axis=0, keepdims=True)

    def axial_synthesis(field):
        for chunk in range(2):
            modes = []
            for parity in range(2):
                for part in range(2):
                    axes = slice(32 * part, 32 * (part + 1))
                    lanes = [
                        in_ref[axes, 2 * chunk + k, field, parity].reshape(QUARTER, 128)
                        for k in range(2)
                    ]
                    modes.append(jnp.concatenate(lanes, axis=1))
            ec, es, oc, os = (
                product((out_table_ref[t, 0], out_table_ref[t, 1]), split(modes[t]))
                for t in range(4)
            )
            nyquist = modes[1][0:1] * unit
            middle = total(modes[0] * scale) + nyquist
            ec = ec + sign * nyquist
            even = ec + es, jnp.where(zero, middle, ec - es)
            odd = jnp.where(zero, oc, os + oc), jnp.where(zero, os, os - oc)
            columns = pl.ds(256 * chunk, 256)
            blocks = even[0] + odd[0], even[1] + odd[1], even[0] - odd[0], even[1] - odd[1]
            for k, value in enumerate(blocks):
                rows = pl.ds(QUARTER * k, QUARTER)
                high_ref[rows, columns], low_ref[rows, columns] = split(value)
                if chunk == 0:
                    middle_ref[rows, 0:1] = line_total(value * lane_scale)
                else:
                    nyquist_ref[rows, 0:1] = value[:, 0:1] * lane_unit

    cosine_lanes, sine_lanes = pl.ds(0, 256), pl.ds(256, 256)

    def azimuth_synthesis(k):
        rows = pl.ds(HALF * k, HALF)
        cosines, sines = (
            product(
                (high_ref[rows, lanes], low_ref[rows, lanes]),
                (line_out_ref[t, 0], line_out_ref[t, 1]),
            )
            for t, lanes in enumerate((cosine_lanes, sine_lanes))
        )
        nyquist = nyquist_ref[rows, 0:1]
        cosines = cosines + lane_sign * nyquist
        middle = middle_ref[rows, 0:1] + nyquist
        return cosines + sines, jnp.where(lane_zero, middle, cosines - sines)

    axial_synthesis(0)
    for k in range(2):
        rows = pl.ds(HALF * k, HALF)
        state_ref[rows, cosine_lanes], state_ref[rows, sine_lanes] = azimuth_synthesis(k)
    axial_synthesis(1)
    for k in range(2):
        rows = pl.ds(HALF * k, HALF)
        for lanes, adjoint in zip((cosine_lanes, sine_lanes), azimuth_synthesis(k)):
            state = state_ref[rows, lanes]
            state_ref[rows, lanes] = (3.0 * state * state - 1.0) * adjoint

    root = math.sqrt(2.0)

    def back(t, x):
        return product((back_table_ref[t, 0], back_table_ref[t, 1]), split(x))

    for parity in range(2):
        lines = []
        for chunk in range(2):
            columns = pl.ds(256 * chunk, 256)
            w = [state_ref[pl.ds(QUARTER * k, QUARTER), columns] for k in range(4)]
            if parity == 0:
                upper, lower = w[0] + w[2], w[1] + w[3]
                middle = lower[0:1]
                folded = jnp.where(zero, upper, upper + lower)
                cosines = back(0, folded) + (root * scale) * middle
                nyquist = (root * unit) * (total(sign * folded) + middle)
                sines = jnp.where(zero, nyquist, back(1, upper - lower))
            else:
                upper, lower = w[0] - w[2], w[1] - w[3]
                cosines = back(2, jnp.where(zero, upper, upper - lower))
                sines = back(3, jnp.where(zero, lower, upper + lower))
            lines.append((cosines, sines))
        for part in range(2):
            upper, lower = lines[0][part], lines[1][part]
            middle = lower[:, 0:1]
            folded = jnp.where(lane_zero, upper, upper + lower)
            cosines = product(split(folded), (line_back_ref[0, 0], line_back_ref[0, 1]))
            cosines = cosines + (lane_scale / root) * middle
            nyquist = (lane_unit / root) * (line_total(lane_sign * folded) + middle)
            sines = product(split(upper - lower), (line_back_ref[1, 0], line_back_ref[1, 1]))
            sines = jnp.where(lane_zero, nyquist, sines)
            for k in range(4):
                value = (cosines, sines)[k // 2][:, 128 * (k % 2) : 128 * (k % 2 + 1)]
                axes = slice(32 * part, 32 * (part + 1))
                out_ref[axes, k, parity] = value.reshape(32, 8, 128)


def params(mebibytes):
    return pltpu.CompilerParams(vmem_limit_bytes=mebibytes * 2**20)


NEAR = pl.BlockSpec(memory_space=pltpu.VMEM)


FAR = pl.BlockSpec(memory_space=pl.ANY)


def far(x):
    return pltpu.with_memory_space_constraint(x, pltpu.HBM)


def near_shape(*dims):
    return pltpu.VMEM(dims, jnp.float32)


def run_radial_out(phase_field, section_cotangent):
    c = halves(np.ascontiguousarray(radial_table(NR).T))
    return pl.pallas_call(
        radial_out,
        in_specs=[FAR] * 4,
        out_specs=NEAR,
        out_shape=near_shape(NR, 32, 128),
        scratch_shapes=[
            pltpu.VMEM((4, 8, NR, 128), jnp.float32),
            pltpu.VMEM((4, NR, 8, 128), jnp.float32),
            pltpu.VMEM((2, NR, NR), jnp.bfloat16),
            pltpu.SemaphoreType.DMA((6,)),
        ],
        compiler_params=params(20),
        name="radial_out",
    )(*(far(x.reshape(8, 2, NR, 128)) for x in (phase_field, section_cotangent)), *map(far, c))


def run_grid(taken):
    tables = []
    for group, factor in ((azimuth_tables(), math.sqrt(0.5)), (axial_tables(), math.sqrt(2.0))):
        tables.append(np.stack([np.stack(halves(t)) for t in group]))
        tables.append(np.stack([np.stack(halves(t.T * factor)) for t in group]))
    return pl.pallas_call(
        grid_kernel,
        in_specs=[NEAR] * 5,
        out_specs=NEAR,
        out_shape=near_shape(64, 4, 2, 8, 128),
        scratch_shapes=[
            pltpu.VMEM((NX, NY), jnp.bfloat16),
            pltpu.VMEM((NX, NY), jnp.bfloat16),
            pltpu.VMEM((NX, NY), jnp.float32),
            pltpu.VMEM((NX, 128), jnp.float32),
            pltpu.VMEM((NX, 128), jnp.float32),
        ],
        compiler_params=params(30),
        name="grid",
    )(taken.reshape(64, 4, 2, 2, 8, 128), *tables)


def run_radial_back(back):
    c = halves(radial_table(NR))
    return pl.pallas_call(
        radial_back,
        in_specs=[NEAR] * 3,
        out_specs=FAR,
        out_shape=jax.ShapeDtypeStruct((8, 2, NR, 128), jnp.float32),
        scratch_shapes=[pltpu.VMEM((2, 8, NR, 128), jnp.float32), pltpu.SemaphoreType.DMA((8,))],
        compiler_params=params(14),
        name="radial_back",
    )(back, *c).reshape(16, NR, 128)


def exchange(x):
    return lax.all_to_all(x, BOTH, split_axis=0, concat_axis=0, tiled=True)


def per_device(phase_field, section_cotangent):
    taken = exchange(run_radial_out(phase_field, section_cotangent))
    back = exchange(run_grid(taken).reshape(NR, 16, 128))
    return run_radial_back(back)


def solution(mesh):
    spec = P("ax", None, "az")
    return jax.shard_map(
        per_device, mesh=mesh, in_specs=(spec, spec), out_specs=spec, check_vma=False
    )
```

```python
import functools
import math

import jax
import jax.numpy as jnp
import ml_dtypes
import numpy as np
from jax import lax
from jax.experimental import pallas as pl
from jax.experimental.pallas import tpu as pltpu
from jax.sharding import PartitionSpec as P

NX = 1024
NY = 512
NR = 256
BOTH = ("ax", "az")


def halves(table):
    high = table.astype(ml_dtypes.bfloat16)
    low = (table - high.astype(np.float64)).astype(ml_dtypes.bfloat16)
    return high, low


def fourier_table(count):
    modes = np.arange(count)[:, None]
    points = np.arange(count)[None, :]
    half = count // 2
    wave = np.where(modes <= half, modes, modes - half)
    angle = 2.0 * math.pi / count * (wave * points % count)
    scale = np.where((modes == 0) | (modes == half), math.sqrt(1.0 / count), math.sqrt(2.0 / count))
    return scale * np.where(modes <= half, np.cos(angle), np.sin(angle))


def radial_table(count):
    modes = np.arange(count)[:, None]
    points = np.arange(count)[None, :]
    weight = np.where(modes == 0, math.sqrt(1.0 / count), math.sqrt(2.0 / count))
    return weight * np.cos(math.pi * modes * (points + 0.5) / count)


def split(x):
    high = x.astype(jnp.bfloat16)
    low = (x - high.astype(jnp.float32)).astype(jnp.bfloat16)
    return high, low


def dot(a, b):
    return lax.dot_general(a, b, (((1,), (0,)), ((), ())), preferred_element_type=jnp.float32)


def product(a, b):
    return dot(jnp.concatenate([a[0], a[0], a[1]], 1), jnp.concatenate([b[0], b[1], b[0]], 0))


HALF = NX // 2
QUARTER = NX // 4


def radial_out(s_hbm, a_hbm, th_hbm, tl_hbm, out_ref, x_ref, turn_ref, table_ref, sems):
    tables = [
        pltpu.make_async_copy(th_hbm, table_ref.at[0], sems.at[3]),
        pltpu.make_async_copy(tl_hbm, table_ref.at[1], sems.at[4]),
    ]
    loads = {
        (0, 0): pltpu.make_async_copy(s_hbm.at[0:4], x_ref.at[0, 0:4], sems.at[0]),
        (0, 4): pltpu.make_async_copy(s_hbm.at[4:8], x_ref.at[0, 4:8], sems.at[1]),
        (1, 0): pltpu.make_async_copy(a_hbm, x_ref.at[1], sems.at[2]),
    }
    for copy in (*tables, *loads.values()):
        copy.start()
    for copy in tables:
        copy.wait()
    table = table_ref[0], table_ref[1]

    def turn(field, first, last):
        for group in (2 * field, 2 * field + 1):
            rows = slice(8 * group, 8 * (group + 1))
            out_ref[first:last, rows, :] = turn_ref[group, first:last]

    for field in range(2):
        for i in range(8):
            if (field, i) in loads:
                loads[field, i].wait()
            pair = jnp.concatenate([x_ref[field, i, 0], x_ref[field, i, 1]], axis=1)
            result = product(table, split(pair))
            for parity in range(2):
                rows = turn_ref.at[2 * field + parity].reshape(NR * 8, 128)
                rows[pl.ds(i, NR, stride=8), :] = result[:, 128 * parity : 128 * (parity + 1)]
            if field == 1:
                turn(0, 32 * i, 32 * (i + 1))
    turn(1, 0, NR)


def radial_back(in_ref, th_ref, tl_ref, out_hbm, out_ref, sems):
    table = th_ref[...], tl_ref[...]
    rows = in_ref.reshape(NR * 16, 128)
    stores = []
    for parity in range(2):
        for i in range(0, 8, 2):
            lanes = [rows[pl.ds(8 * parity + i + k, NR, stride=16), :] for k in range(2)]
            result = product(table, split(jnp.concatenate(lanes, axis=1)))
            for k in range(2):
                out_ref[parity, i + k] = result[:, 128 * k : 128 * (k + 1)]
            stores.append(
                pltpu.make_async_copy(
                    out_ref.at[parity, i : i + 2], out_hbm.at[i : i + 2, parity],
                    sems.at[4 * parity + i // 2],
                )
            )
            stores[-1].start()
    for store in stores:
        store.wait()


def axial_tables():
    axial = fourier_table(NX)
    r = np.arange(QUARTER)
    turned = np.where(r == 0, QUARTER, r)
    even, odd = axial[0::2], axial[1::2]
    even_sines = even[QUARTER:, :QUARTER].T.copy()
    even_sines[:, 0] = 0.0
    return even[:QUARTER, :QUARTER].T, even_sines, odd[:QUARTER, :QUARTER].T, odd[QUARTER:][:, turned].T


def azimuth_tables():
    table = fourier_table(NY)
    half = NY // 2
    sines = table[half:, :half].copy()
    sines[0] = 0.0
    return table[:half, :half], sines


def grid_kernel(
    in_ref, line_out_ref, line_back_ref, out_table_ref, back_table_ref, out_ref,
    high_ref, low_ref, state_ref, middle_ref, nyquist_ref,
):
    index = lax.broadcasted_iota(jnp.int32, (QUARTER, 256), 0)
    zero = index == 0
    sign = jnp.where(index % 2 == 0, 1.0, -1.0)
    unit = math.sqrt(1.0 / NX)
    scale = sign * jnp.where(zero, unit, math.sqrt(2.0) * unit)

    lane = lax.broadcasted_iota(jnp.int32, (1, 256), 1)
    lane_zero = lane == 0
    lane_sign = jnp.where(lane % 2 == 0, 1.0, -1.0)
    lane_unit = math.sqrt(1.0 / NY)
    lane_scale = lane_sign * jnp.where(lane_zero, lane_unit, math.sqrt(2.0) * lane_unit)

    def line_total(x):
        return jnp.sum(x, axis=1, keepdims=True)

    def total(x):
        return jnp.sum(x, axis=0, keepdims=True)

    def axial_synthesis(field):
        for chunk in range(2):
            modes = []
            for parity in range(2):
                for part in range(2):
                    axes = slice(32 * part, 32 * (part + 1))
                    lanes = [
                        in_ref[axes, 2 * chunk + k, field, parity].reshape(QUARTER, 128)
                        for k in range(2)
                    ]
                    modes.append(jnp.concatenate(lanes, axis=1))
            ec, es, oc, os = (
                product((out_table_ref[t, 0], out_table_ref[t, 1]), split(modes[t]))
                for t in range(4)
            )
            nyquist = modes[1][0:1] * unit
            middle = total(modes[0] * scale) + nyquist
            ec = ec + sign * nyquist
            even = ec + es, jnp.where(zero, middle, ec - es)
            odd = jnp.where(zero, oc, os + oc), jnp.where(zero, os, os - oc)
            columns = pl.ds(256 * chunk, 256)
            blocks = even[0] + odd[0], even[1] + odd[1], even[0] - odd[0], even[1] - odd[1]
            for k, value in enumerate(blocks):
                rows = pl.ds(QUARTER * k, QUARTER)
                high_ref[rows, columns], low_ref[rows, columns] = split(value)
                if chunk == 0:
                    middle_ref[rows, 0:1] = line_total(value * lane_scale)
                else:
                    nyquist_ref[rows, 0:1] = value[:, 0:1] * lane_unit

    cosine_lanes, sine_lanes = pl.ds(0, 256), pl.ds(256, 256)

    def azimuth_synthesis(k):
        rows = pl.ds(HALF * k, HALF)
        cosines, sines = (
            product(
                (high_ref[rows, lanes], low_ref[rows, lanes]),
                (line_out_ref[t, 0], line_out_ref[t, 1]),
            )
            for t, lanes in enumerate((cosine_lanes, sine_lanes))
        )
        nyquist = nyquist_ref[rows, 0:1]
        cosines = cosines + lane_sign * nyquist
        middle = middle_ref[rows, 0:1] + nyquist
        return cosines + sines, jnp.where(lane_zero, middle, cosines - sines)

    axial_synthesis(0)
    for k in range(2):
        rows = pl.ds(HALF * k, HALF)
        state_ref[rows, cosine_lanes], state_ref[rows, sine_lanes] = azimuth_synthesis(k)
    axial_synthesis(1)
    for k in range(2):
        rows = pl.ds(HALF * k, HALF)
        for lanes, adjoint in zip((cosine_lanes, sine_lanes), azimuth_synthesis(k)):
            state = state_ref[rows, lanes]
            state_ref[rows, lanes] = (3.0 * state * state - 1.0) * adjoint

    root = math.sqrt(2.0)

    def back(t, x):
        return product((back_table_ref[t, 0], back_table_ref[t, 1]), split(x))

    for parity in range(2):
        lines = []
        for chunk in range(2):
            columns = pl.ds(256 * chunk, 256)
            w = [state_ref[pl.ds(QUARTER * k, QUARTER), columns] for k in range(4)]
            if parity == 0:
                upper, lower = w[0] + w[2], w[1] + w[3]
                middle = lower[0:1]
                folded = jnp.where(zero, upper, upper + lower)
                cosines = back(0, folded) + (root * scale) * middle
                nyquist = (root * unit) * (total(sign * folded) + middle)
                sines = jnp.where(zero, nyquist, back(1, upper - lower))
            else:
                upper, lower = w[0] - w[2], w[1] - w[3]
                cosines = back(2, jnp.where(zero, upper, upper - lower))
                sines = back(3, jnp.where(zero, lower, upper + lower))
            lines.append((cosines, sines))
        for part in range(2):
            upper, lower = lines[0][part], lines[1][part]
            middle = lower[:, 0:1]
            folded = jnp.where(lane_zero, upper, upper + lower)
            cosines = product(split(folded), (line_back_ref[0, 0], line_back_ref[0, 1]))
            cosines = cosines + (lane_scale / root) * middle
            nyquist = (lane_unit / root) * (line_total(lane_sign * folded) + middle)
            sines = product(split(upper - lower), (line_back_ref[1, 0], line_back_ref[1, 1]))
            sines = jnp.where(lane_zero, nyquist, sines)
            for k in range(4):
                value = (cosines, sines)[k // 2][:, 128 * (k % 2) : 128 * (k % 2 + 1)]
                axes = slice(32 * part, 32 * (part + 1))
                out_ref[axes, k, parity] = value.reshape(32, 8, 128)


def params(mebibytes):
    return pltpu.CompilerParams(vmem_limit_bytes=mebibytes * 2**20)


NEAR = pl.BlockSpec(memory_space=pltpu.VMEM)


FAR = pl.BlockSpec(memory_space=pl.ANY)


def far(x):
    return pltpu.with_memory_space_constraint(x, pltpu.HBM)


def near_shape(*dims):
    return pltpu.VMEM(dims, jnp.float32)


def run_radial_out(phase_field, section_cotangent):
    c = halves(np.ascontiguousarray(radial_table(NR).T))
    return pl.pallas_call(
        radial_out,
        in_specs=[FAR] * 4,
        out_specs=NEAR,
        out_shape=near_shape(NR, 32, 128),
        scratch_shapes=[
            pltpu.VMEM((2, 8, 2, NR, 128), jnp.float32),
            pltpu.VMEM((4, NR, 8, 128), jnp.float32),
            pltpu.VMEM((2, NR, NR), jnp.bfloat16),
            pltpu.SemaphoreType.DMA((5,)),
        ],
        compiler_params=params(20),
        name="radial_out",
    )(*(far(x.reshape(8, 2, NR, 128)) for x in (phase_field, section_cotangent)), *map(far, c))


def run_grid(taken):
    tables = []
    for group, factor in ((azimuth_tables(), math.sqrt(0.5)), (axial_tables(), math.sqrt(2.0))):
        tables.append(np.stack([np.stack(halves(t)) for t in group]))
        tables.append(np.stack([np.stack(halves(t.T * factor)) for t in group]))
    return pl.pallas_call(
        grid_kernel,
        in_specs=[NEAR] * 5,
        out_specs=NEAR,
        out_shape=near_shape(64, 4, 2, 8, 128),
        scratch_shapes=[
            pltpu.VMEM((NX, NY), jnp.bfloat16),
            pltpu.VMEM((NX, NY), jnp.bfloat16),
            pltpu.VMEM((NX, NY), jnp.float32),
            pltpu.VMEM((NX, 128), jnp.float32),
            pltpu.VMEM((NX, 128), jnp.float32),
        ],
        compiler_params=params(30),
        name="grid",
    )(taken.reshape(64, 4, 2, 2, 8, 128), *tables)


def run_radial_back(back):
    c = halves(radial_table(NR))
    return pl.pallas_call(
        radial_back,
        in_specs=[NEAR] * 3,
        out_specs=FAR,
        out_shape=jax.ShapeDtypeStruct((8, 2, NR, 128), jnp.float32),
        scratch_shapes=[pltpu.VMEM((2, 8, NR, 128), jnp.float32), pltpu.SemaphoreType.DMA((8,))],
        compiler_params=params(14),
        name="radial_back",
    )(back, *c).reshape(16, NR, 128)


def exchange(x):
    return lax.all_to_all(x, BOTH, split_axis=0, concat_axis=0, tiled=True)


def per_device(phase_field, section_cotangent):
    taken = exchange(run_radial_out(phase_field, section_cotangent))
    back = exchange(run_grid(taken).reshape(NR, 16, 128))
    return run_radial_back(back)


def solution(mesh):
    spec = P("ax", None, "az")
    return jax.shard_map(
        per_device, mesh=mesh, in_specs=(spec, spec), out_specs=spec, check_vma=False
    )
```

```python
import functools
import math

import jax
import jax.numpy as jnp
import ml_dtypes
import numpy as np
from jax import lax
from jax.experimental import pallas as pl
from jax.experimental.pallas import tpu as pltpu
from jax.sharding import Mesh, PartitionSpec as P

NX = 1024
NY = 512
NR = 256
AXES = ("x", "y", "zl", "core", "zh")
ORDER = ("x", "y", "zh", "zl", "core")


def halves(table):
    high = table.astype(ml_dtypes.bfloat16)
    low = (table - high.astype(np.float64)).astype(ml_dtypes.bfloat16)
    return high, low


def fourier_table(count):
    modes = np.arange(count)[:, None]
    points = np.arange(count)[None, :]
    half = count // 2
    wave = np.where(modes <= half, modes, modes - half)
    angle = 2.0 * math.pi / count * (wave * points % count)
    scale = np.where((modes == 0) | (modes == half), math.sqrt(1.0 / count), math.sqrt(2.0 / count))
    return scale * np.where(modes <= half, np.cos(angle), np.sin(angle))


def radial_table(count):
    modes = np.arange(count)[:, None]
    points = np.arange(count)[None, :]
    weight = np.where(modes == 0, math.sqrt(1.0 / count), math.sqrt(2.0 / count))
    return weight * np.cos(math.pi * modes * (points + 0.5) / count)


def split(x):
    high = x.astype(jnp.bfloat16)
    low = (x - high.astype(jnp.float32)).astype(jnp.bfloat16)
    return high, low


def dot(a, b):
    return lax.dot_general(a, b, (((1,), (0,)), ((), ())), preferred_element_type=jnp.float32)


def product(a, b):
    return dot(jnp.concatenate([a[0], a[0], a[1]], 1), jnp.concatenate([b[0], b[1], b[0]], 0))


HALF = NX // 2
QUARTER = NX // 4


def radial_out(s_hbm, a_hbm, th_hbm, tl_hbm, out_ref, x_ref, turn_ref, table_ref, sems):
    tables = [
        pltpu.make_async_copy(th_hbm, table_ref.at[0], sems.at[3]),
        pltpu.make_async_copy(tl_hbm, table_ref.at[1], sems.at[4]),
    ]
    loads = {
        (0, 0): pltpu.make_async_copy(s_hbm.at[0:4], x_ref.at[0, 0:4], sems.at[0]),
        (0, 4): pltpu.make_async_copy(s_hbm.at[4:8], x_ref.at[0, 4:8], sems.at[1]),
        (1, 0): pltpu.make_async_copy(a_hbm, x_ref.at[1], sems.at[2]),
    }
    for copy in (*tables, *loads.values()):
        copy.start()
    for copy in tables:
        copy.wait()
    table = table_ref[0], table_ref[1]

    def turn(field, first, last):
        for group in (2 * field, 2 * field + 1):
            rows = slice(8 * group, 8 * (group + 1))
            out_ref[first:last, rows, :] = turn_ref[group, first:last]

    for field in range(2):
        for i in range(8):
            if (field, i) in loads:
                loads[field, i].wait()
            pair = jnp.concatenate([x_ref[field, i, 0], x_ref[field, i, 1]], axis=1)
            result = product(table, split(pair))
            for parity in range(2):
                rows = turn_ref.at[2 * field + parity].reshape(NR * 8, 128)
                rows[pl.ds(i, NR, stride=8), :] = result[:, 128 * parity : 128 * (parity + 1)]
            if field == 1:
                turn(0, 32 * i, 32 * (i + 1))
    turn(1, 0, NR)


def radial_back(in_ref, th_ref, tl_ref, out_hbm, out_ref, sems):
    table = th_ref[...], tl_ref[...]
    rows = in_ref.reshape(NR * 16, 128)
    stores = []
    for parity in range(2):
        for i in range(0, 8, 2):
            lanes = [rows[pl.ds(8 * parity + i + k, NR, stride=16), :] for k in range(2)]
            result = product(table, split(jnp.concatenate(lanes, axis=1)))
            for k in range(2):
                out_ref[parity, i + k] = result[:, 128 * k : 128 * (k + 1)]
            stores.append(
                pltpu.make_async_copy(
                    out_ref.at[parity, i : i + 2], out_hbm.at[i : i + 2, parity],
                    sems.at[4 * parity + i // 2],
                )
            )
            stores[-1].start()
    for store in stores:
        store.wait()


def axial_tables():
    axial = fourier_table(NX)
    r = np.arange(QUARTER)
    turned = np.where(r == 0, QUARTER, r)
    even, odd = axial[0::2], axial[1::2]
    even_sines = even[QUARTER:, :QUARTER].T.copy()
    even_sines[:, 0] = 0.0
    return even[:QUARTER, :QUARTER].T, even_sines, odd[:QUARTER, :QUARTER].T, odd[QUARTER:][:, turned].T


def azimuth_tables():
    table = fourier_table(NY)
    half = NY // 2
    sines = table[half:, :half].copy()
    sines[0] = 0.0
    return table[:half, :half], sines


def grid_kernel(
    in_ref, line_out_ref, line_back_ref, out_table_ref, back_table_ref, out_ref,
    high_ref, low_ref, state_ref, middle_ref, nyquist_ref,
):
    index = lax.broadcasted_iota(jnp.int32, (QUARTER, 256), 0)
    zero = index == 0
    sign = jnp.where(index % 2 == 0, 1.0, -1.0)
    unit = math.sqrt(1.0 / NX)
    scale = sign * jnp.where(zero, unit, math.sqrt(2.0) * unit)

    lane = lax.broadcasted_iota(jnp.int32, (1, 256), 1)
    lane_zero = lane == 0
    lane_sign = jnp.where(lane % 2 == 0, 1.0, -1.0)
    lane_unit = math.sqrt(1.0 / NY)
    lane_scale = lane_sign * jnp.where(lane_zero, lane_unit, math.sqrt(2.0) * lane_unit)

    def line_total(x):
        return jnp.sum(x, axis=1, keepdims=True)

    def total(x):
        return jnp.sum(x, axis=0, keepdims=True)

    def axial_synthesis(field):
        for chunk in range(2):
            modes = []
            for parity in range(2):
                for part in range(2):
                    axes = slice(8 * part, 8 * (part + 1))
                    lanes = [
                        in_ref[axes, 2 * chunk + k, :, field, parity].reshape(QUARTER, 128)
                        for k in range(2)
                    ]
                    modes.append(jnp.concatenate(lanes, axis=1))
            ec, es, oc, os = (
                product((out_table_ref[t, 0], out_table_ref[t, 1]), split(modes[t]))
                for t in range(4)
            )
            nyquist = modes[1][0:1] * unit
            middle = total(modes[0] * scale) + nyquist
            ec = ec + sign * nyquist
            even = ec + es, jnp.where(zero, middle, ec - es)
            odd = jnp.where(zero, oc, os + oc), jnp.where(zero, os, os - oc)
            columns = pl.ds(256 * chunk, 256)
            blocks = even[0] + odd[0], even[1] + odd[1], even[0] - odd[0], even[1] - odd[1]
            for k, value in enumerate(blocks):
                rows = pl.ds(QUARTER * k, QUARTER)
                high_ref[rows, columns], low_ref[rows, columns] = split(value)
                if chunk == 0:
                    middle_ref[rows, 0:1] = line_total(value * lane_scale)
                else:
                    nyquist_ref[rows, 0:1] = value[:, 0:1] * lane_unit

    cosine_lanes, sine_lanes = pl.ds(0, 256), pl.ds(256, 256)

    def azimuth_synthesis(k):
        rows = pl.ds(HALF * k, HALF)
        cosines, sines = (
            product(
                (high_ref[rows, lanes], low_ref[rows, lanes]),
                (line_out_ref[t, 0], line_out_ref[t, 1]),
            )
            for t, lanes in enumerate((cosine_lanes, sine_lanes))
        )
        nyquist = nyquist_ref[rows, 0:1]
        cosines = cosines + lane_sign * nyquist
        middle = middle_ref[rows, 0:1] + nyquist
        return cosines + sines, jnp.where(lane_zero, middle, cosines - sines)

    axial_synthesis(0)
    for k in range(2):
        rows = pl.ds(HALF * k, HALF)
        state_ref[rows, cosine_lanes], state_ref[rows, sine_lanes] = azimuth_synthesis(k)
    axial_synthesis(1)
    for k in range(2):
        rows = pl.ds(HALF * k, HALF)
        for lanes, adjoint in zip((cosine_lanes, sine_lanes), azimuth_synthesis(k)):
            state = state_ref[rows, lanes]
            state_ref[rows, lanes] = (3.0 * state * state - 1.0) * adjoint

    root = math.sqrt(2.0)

    def back(t, x):
        return product((back_table_ref[t, 0], back_table_ref[t, 1]), split(x))

    for parity in range(2):
        lines = []
        for chunk in range(2):
            columns = pl.ds(256 * chunk, 256)
            w = [state_ref[pl.ds(QUARTER * k, QUARTER), columns] for k in range(4)]
            if parity == 0:
                upper, lower = w[0] + w[2], w[1] + w[3]
                middle = lower[0:1]
                folded = jnp.where(zero, upper, upper + lower)
                cosines = back(0, folded) + (root * scale) * middle
                nyquist = (root * unit) * (total(sign * folded) + middle)
                sines = jnp.where(zero, nyquist, back(1, upper - lower))
            else:
                upper, lower = w[0] - w[2], w[1] - w[3]
                cosines = back(2, jnp.where(zero, upper, upper - lower))
                sines = back(3, jnp.where(zero, lower, upper + lower))
            lines.append((cosines, sines))
        for part in range(2):
            upper, lower = lines[0][part], lines[1][part]
            middle = lower[:, 0:1]
            folded = jnp.where(lane_zero, upper, upper + lower)
            cosines = product(split(folded), (line_back_ref[0, 0], line_back_ref[0, 1]))
            cosines = cosines + (lane_scale / root) * middle
            nyquist = (lane_unit / root) * (line_total(lane_sign * folded) + middle)
            sines = product(split(upper - lower), (line_back_ref[1, 0], line_back_ref[1, 1]))
            sines = jnp.where(lane_zero, nyquist, sines)
            for k in range(4):
                value = (cosines, sines)[k // 2][:, 128 * (k % 2) : 128 * (k % 2 + 1)]
                axes = slice(8 * part, 8 * (part + 1))
                out_ref[axes, k, :, parity] = value.reshape(8, 4, 8, 128)


def params(mebibytes):
    return pltpu.CompilerParams(vmem_limit_bytes=mebibytes * 2**20)


NEAR = pl.BlockSpec(memory_space=pltpu.VMEM)


FAR = pl.BlockSpec(memory_space=pl.ANY)


def far(x):
    return pltpu.with_memory_space_constraint(x, pltpu.HBM)


def near_shape(*dims):
    return pltpu.VMEM(dims, jnp.float32)


def run_radial_out(phase_field, section_cotangent):
    c = halves(np.ascontiguousarray(radial_table(NR).T))
    return pl.pallas_call(
        radial_out,
        in_specs=[FAR] * 4,
        out_specs=NEAR,
        out_shape=near_shape(NR, 32, 128),
        scratch_shapes=[
            pltpu.VMEM((2, 8, 2, NR, 128), jnp.float32),
            pltpu.VMEM((4, NR, 8, 128), jnp.float32),
            pltpu.VMEM((2, NR, NR), jnp.bfloat16),
            pltpu.SemaphoreType.DMA((5,)),
        ],
        compiler_params=params(20),
        name="radial_out",
    )(*(far(x.reshape(8, 2, NR, 128)) for x in (phase_field, section_cotangent)), *map(far, c))


def run_grid(taken):
    tables = []
    for group, factor in ((azimuth_tables(), math.sqrt(0.5)), (axial_tables(), math.sqrt(2.0))):
        tables.append(np.stack([np.stack(halves(t)) for t in group]))
        tables.append(np.stack([np.stack(halves(t.T * factor)) for t in group]))
    return pl.pallas_call(
        grid_kernel,
        in_specs=[NEAR] * 5,
        out_specs=NEAR,
        out_shape=near_shape(16, 4, 4, 2, 8, 128),
        scratch_shapes=[
            pltpu.VMEM((NX, NY), jnp.bfloat16),
            pltpu.VMEM((NX, NY), jnp.bfloat16),
            pltpu.VMEM((NX, NY), jnp.float32),
            pltpu.VMEM((NX, 128), jnp.float32),
            pltpu.VMEM((NX, 128), jnp.float32),
        ],
        compiler_params=params(30),
        name="grid",
    )(taken.reshape(16, 4, 4, 2, 2, 8, 128), *tables)


def run_radial_back(back):
    c = halves(radial_table(NR))
    return pl.pallas_call(
        radial_back,
        in_specs=[NEAR] * 3,
        out_specs=FAR,
        out_shape=jax.ShapeDtypeStruct((8, 2, NR, 128), jnp.float32),
        scratch_shapes=[pltpu.VMEM((2, 8, NR, 128), jnp.float32), pltpu.SemaphoreType.DMA((8,))],
        compiler_params=params(14),
        name="radial_back",
    )(back, *c).reshape(16, NR, 128)


def exchange(x):
    return lax.all_to_all(x, ORDER, split_axis=0, concat_axis=0, tiled=True)


def per_device(phase_field, section_cotangent):
    taken = exchange(run_radial_out(phase_field, section_cotangent))
    back = exchange(run_grid(taken).reshape(NR, 16, 128))
    return run_radial_back(back)


def solution(mesh):
    names = Mesh(mesh.devices.reshape(4, 4, 2, 2, 4), AXES)
    spec = P(("x", "y", "zl", "core"), None, "zh")
    return jax.shard_map(
        per_device, mesh=names, in_specs=(spec, spec), out_specs=spec, check_vma=False
    )
```

```python
import functools
import math

import jax
import jax.numpy as jnp
import ml_dtypes
import numpy as np
from jax import lax
from jax.experimental import pallas as pl
from jax.experimental.pallas import tpu as pltpu
from jax.sharding import Mesh, PartitionSpec as P

NX = 1024
NY = 512
NR = 256
AXES = ("x", "y", "zl", "core", "zh")
ORDER = ("x", "y", "zh", "zl", "core")


def halves(table):
    high = table.astype(ml_dtypes.bfloat16)
    low = (table - high.astype(np.float64)).astype(ml_dtypes.bfloat16)
    return high, low


def fourier_table(count):
    modes = np.arange(count)[:, None]
    points = np.arange(count)[None, :]
    half = count // 2
    wave = np.where(modes <= half, modes, modes - half)
    angle = 2.0 * math.pi / count * (wave * points % count)
    scale = np.where((modes == 0) | (modes == half), math.sqrt(1.0 / count), math.sqrt(2.0 / count))
    return scale * np.where(modes <= half, np.cos(angle), np.sin(angle))


def radial_table(count):
    modes = np.arange(count)[:, None]
    points = np.arange(count)[None, :]
    weight = np.where(modes == 0, math.sqrt(1.0 / count), math.sqrt(2.0 / count))
    return weight * np.cos(math.pi * modes * (points + 0.5) / count)


def split(x):
    high = x.astype(jnp.bfloat16)
    low = (x - high.astype(jnp.float32)).astype(jnp.bfloat16)
    return high, low


def dot(a, b):
    return lax.dot_general(a, b, (((1,), (0,)), ((), ())), preferred_element_type=jnp.float32)


def product(a, b):
    return dot(jnp.concatenate([a[0], a[0], a[1]], 1), jnp.concatenate([b[0], b[1], b[0]], 0))


HALF = NX // 2
QUARTER = NX // 4


def radial_out(s_hbm, a_hbm, th_hbm, tl_hbm, out_ref, x_ref, turn_ref, table_ref, sems):
    tables = [
        pltpu.make_async_copy(th_hbm, table_ref.at[0], sems.at[3]),
        pltpu.make_async_copy(tl_hbm, table_ref.at[1], sems.at[4]),
    ]
    loads = {
        (0, 0): pltpu.make_async_copy(s_hbm.at[0:4], x_ref.at[0, 0:4], sems.at[0]),
        (0, 4): pltpu.make_async_copy(s_hbm.at[4:8], x_ref.at[0, 4:8], sems.at[1]),
        (1, 0): pltpu.make_async_copy(a_hbm, x_ref.at[1], sems.at[2]),
    }
    for copy in (*tables, *loads.values()):
        copy.start()
    for copy in tables:
        copy.wait()
    table = table_ref[0], table_ref[1]

    def turn(group, first, last):
        out_ref[first:last, 8 * group : 8 * (group + 1), :] = turn_ref[group, first:last]

    def synthesize(field, places):
        pair = jnp.concatenate([x_ref[field, i, parity] for i, parity in places], axis=1)
        result = product(table, split(pair))
        for k, (i, parity) in enumerate(places):
            rows = turn_ref.at[2 * field + parity].reshape(NR * 8, 128)
            rows[pl.ds(i, NR, stride=8), :] = result[:, 128 * k : 128 * (k + 1)]

    for i in range(8):
        if (0, i) in loads:
            loads[0, i].wait()
        synthesize(0, ((i, 0), (i, 1)))
    loads[1, 0].wait()
    for parity in range(2):
        for i in range(0, 8, 2):
            synthesize(1, ((i, parity), (i + 1, parity)))
            first = 32 * i
            if parity == 0:
                turn(0, first, first + 64)
                turn(1, first, first + 64)
            else:
                turn(2, first, first + 64)
    turn(3, 0, NR)


def radial_back(in_ref, th_ref, tl_ref, out_hbm, out_ref, sems):
    table = th_ref[...], tl_ref[...]
    rows = in_ref.reshape(NR * 16, 128)
    stores = []
    for parity in range(2):
        for i in range(0, 8, 2):
            lanes = [rows[pl.ds(8 * parity + i + k, NR, stride=16), :] for k in range(2)]
            result = product(table, split(jnp.concatenate(lanes, axis=1)))
            for k in range(2):
                out_ref[parity, i + k] = result[:, 128 * k : 128 * (k + 1)]
            stores.append(
                pltpu.make_async_copy(
                    out_ref.at[parity, i : i + 2], out_hbm.at[i : i + 2, parity],
                    sems.at[4 * parity + i // 2],
                )
            )
            stores[-1].start()
    for store in stores:
        store.wait()


def axial_tables():
    axial = fourier_table(NX)
    r = np.arange(QUARTER)
    turned = np.where(r == 0, QUARTER, r)
    even, odd = axial[0::2], axial[1::2]
    even_sines = even[QUARTER:, :QUARTER].T.copy()
    even_sines[:, 0] = 0.0
    return even[:QUARTER, :QUARTER].T, even_sines, odd[:QUARTER, :QUARTER].T, odd[QUARTER:][:, turned].T


def azimuth_tables():
    table = fourier_table(NY)
    half = NY // 2
    sines = table[half:, :half].copy()
    sines[0] = 0.0
    return table[:half, :half], sines


def grid_kernel(
    in_ref, line_out_ref, line_back_ref, out_table_ref, back_table_ref, out_ref,
    high_ref, low_ref, state_ref, middle_ref, nyquist_ref,
):
    index = lax.broadcasted_iota(jnp.int32, (QUARTER, 256), 0)
    zero = index == 0
    sign = jnp.where(index % 2 == 0, 1.0, -1.0)
    unit = math.sqrt(1.0 / NX)
    scale = sign * jnp.where(zero, unit, math.sqrt(2.0) * unit)

    lane = lax.broadcasted_iota(jnp.int32, (1, 256), 1)
    lane_zero = lane == 0
    lane_sign = jnp.where(lane % 2 == 0, 1.0, -1.0)
    lane_unit = math.sqrt(1.0 / NY)
    lane_scale = lane_sign * jnp.where(lane_zero, lane_unit, math.sqrt(2.0) * lane_unit)

    def line_total(x):
        return jnp.sum(x, axis=1, keepdims=True)

    def total(x):
        return jnp.sum(x, axis=0, keepdims=True)

    def axial_synthesis(field):
        for chunk in range(2):
            modes = []
            for parity in range(2):
                for part in range(2):
                    axes = slice(8 * part, 8 * (part + 1))
                    lanes = [
                        in_ref[axes, 2 * chunk + k, :, field, parity].reshape(QUARTER, 128)
                        for k in range(2)
                    ]
                    modes.append(jnp.concatenate(lanes, axis=1))
            ec, es, oc, os = (
                product((out_table_ref[t, 0], out_table_ref[t, 1]), split(modes[t]))
                for t in range(4)
            )
            nyquist = modes[1][0:1] * unit
            middle = total(modes[0] * scale) + nyquist
            ec = ec + sign * nyquist
            even = ec + es, jnp.where(zero, middle, ec - es)
            odd = jnp.where(zero, oc, os + oc), jnp.where(zero, os, os - oc)
            columns = pl.ds(256 * chunk, 256)
            blocks = even[0] + odd[0], even[1] + odd[1], even[0] - odd[0], even[1] - odd[1]
            for k, value in enumerate(blocks):
                rows = pl.ds(QUARTER * k, QUARTER)
                high_ref[rows, columns], low_ref[rows, columns] = split(value)
                if chunk == 0:
                    middle_ref[rows, 0:1] = line_total(value * lane_scale)
                else:
                    nyquist_ref[rows, 0:1] = value[:, 0:1] * lane_unit

    cosine_lanes, sine_lanes = pl.ds(0, 256), pl.ds(256, 256)

    def azimuth_synthesis(k):
        rows = pl.ds(HALF * k, HALF)
        cosines, sines = (
            product(
                (high_ref[rows, lanes], low_ref[rows, lanes]),
                (line_out_ref[t, 0], line_out_ref[t, 1]),
            )
            for t, lanes in enumerate((cosine_lanes, sine_lanes))
        )
        nyquist = nyquist_ref[rows, 0:1]
        cosines = cosines + lane_sign * nyquist
        middle = middle_ref[rows, 0:1] + nyquist
        return cosines + sines, jnp.where(lane_zero, middle, cosines - sines)

    axial_synthesis(0)
    for k in range(2):
        rows = pl.ds(HALF * k, HALF)
        state_ref[rows, cosine_lanes], state_ref[rows, sine_lanes] = azimuth_synthesis(k)
    axial_synthesis(1)
    for k in range(2):
        rows = pl.ds(HALF * k, HALF)
        for lanes, adjoint in zip((cosine_lanes, sine_lanes), azimuth_synthesis(k)):
            state = state_ref[rows, lanes]
            state_ref[rows, lanes] = (3.0 * state * state - 1.0) * adjoint

    root = math.sqrt(2.0)

    def back(t, x):
        return product((back_table_ref[t, 0], back_table_ref[t, 1]), split(x))

    for parity in range(2):
        lines = []
        for chunk in range(2):
            columns = pl.ds(256 * chunk, 256)
            w = [state_ref[pl.ds(QUARTER * k, QUARTER), columns] for k in range(4)]
            if parity == 0:
                upper, lower = w[0] + w[2], w[1] + w[3]
                middle = lower[0:1]
                folded = jnp.where(zero, upper, upper + lower)
                cosines = back(0, folded) + (root * scale) * middle
                nyquist = (root * unit) * (total(sign * folded) + middle)
                sines = jnp.where(zero, nyquist, back(1, upper - lower))
            else:
                upper, lower = w[0] - w[2], w[1] - w[3]
                cosines = back(2, jnp.where(zero, upper, upper - lower))
                sines = back(3, jnp.where(zero, lower, upper + lower))
            lines.append((cosines, sines))
        for part in range(2):
            upper, lower = lines[0][part], lines[1][part]
            middle = lower[:, 0:1]
            folded = jnp.where(lane_zero, upper, upper + lower)
            cosines = product(split(folded), (line_back_ref[0, 0], line_back_ref[0, 1]))
            cosines = cosines + (lane_scale / root) * middle
            nyquist = (lane_unit / root) * (line_total(lane_sign * folded) + middle)
            sines = product(split(upper - lower), (line_back_ref[1, 0], line_back_ref[1, 1]))
            sines = jnp.where(lane_zero, nyquist, sines)
            for k in range(4):
                value = (cosines, sines)[k // 2][:, 128 * (k % 2) : 128 * (k % 2 + 1)]
                axes = slice(8 * part, 8 * (part + 1))
                out_ref[axes, k, :, parity] = value.reshape(8, 4, 8, 128)


def params(mebibytes):
    return pltpu.CompilerParams(vmem_limit_bytes=mebibytes * 2**20)


NEAR = pl.BlockSpec(memory_space=pltpu.VMEM)


FAR = pl.BlockSpec(memory_space=pl.ANY)


def far(x):
    return pltpu.with_memory_space_constraint(x, pltpu.HBM)


def near_shape(*dims):
    return pltpu.VMEM(dims, jnp.float32)


def run_radial_out(phase_field, section_cotangent):
    c = halves(np.ascontiguousarray(radial_table(NR).T))
    return pl.pallas_call(
        radial_out,
        in_specs=[FAR] * 4,
        out_specs=NEAR,
        out_shape=near_shape(NR, 32, 128),
        scratch_shapes=[
            pltpu.VMEM((2, 8, 2, NR, 128), jnp.float32),
            pltpu.VMEM((4, NR, 8, 128), jnp.float32),
            pltpu.VMEM((2, NR, NR), jnp.bfloat16),
            pltpu.SemaphoreType.DMA((5,)),
        ],
        compiler_params=params(20),
        name="radial_out",
    )(*(far(x.reshape(8, 2, NR, 128)) for x in (phase_field, section_cotangent)), *map(far, c))


def run_grid(taken):
    tables = []
    for group, factor in ((azimuth_tables(), math.sqrt(0.5)), (axial_tables(), math.sqrt(2.0))):
        tables.append(np.stack([np.stack(halves(t)) for t in group]))
        tables.append(np.stack([np.stack(halves(t.T * factor)) for t in group]))
    return pl.pallas_call(
        grid_kernel,
        in_specs=[NEAR] * 5,
        out_specs=NEAR,
        out_shape=near_shape(16, 4, 4, 2, 8, 128),
        scratch_shapes=[
            pltpu.VMEM((NX, NY), jnp.bfloat16),
            pltpu.VMEM((NX, NY), jnp.bfloat16),
            pltpu.VMEM((NX, NY), jnp.float32),
            pltpu.VMEM((NX, 128), jnp.float32),
            pltpu.VMEM((NX, 128), jnp.float32),
        ],
        compiler_params=params(30),
        name="grid",
    )(taken.reshape(16, 4, 4, 2, 2, 8, 128), *tables)


def run_radial_back(back):
    c = halves(radial_table(NR))
    return pl.pallas_call(
        radial_back,
        in_specs=[NEAR] * 3,
        out_specs=FAR,
        out_shape=jax.ShapeDtypeStruct((8, 2, NR, 128), jnp.float32),
        scratch_shapes=[pltpu.VMEM((2, 8, NR, 128), jnp.float32), pltpu.SemaphoreType.DMA((8,))],
        compiler_params=params(14),
        name="radial_back",
    )(back, *c).reshape(16, NR, 128)


def exchange(x):
    return lax.all_to_all(x, ORDER, split_axis=0, concat_axis=0, tiled=True)


def per_device(phase_field, section_cotangent):
    taken = exchange(run_radial_out(phase_field, section_cotangent))
    back = exchange(run_grid(taken).reshape(NR, 16, 128))
    return run_radial_back(back)


def solution(mesh):
    names = Mesh(mesh.devices.reshape(4, 4, 2, 2, 4), AXES)
    spec = P(("x", "y", "zl", "core"), None, "zh")
    return jax.shard_map(
        per_device, mesh=names, in_specs=(spec, spec), out_specs=spec, check_vma=False
    )
```
